256 devices in a mesh: dom: 16 (over y, z_hi, core), orb: 16 (over z_lo, x).
Axes of the slice: x: 4, y: 4, z: 8 (z_hi: 2, z_lo: 4; z = z_hi * 4 + z_lo), core: 2. Of those that a mesh axis runs over, the one named last changes fastest.
Arguments:
- psi: float32 [49152, 2048], P('dom', 'orb'), may hold values from -6 to 6
- rot: float32 [2048, 2048], P(None, 'orb'), may hold values from -0.125 to 0.125
- occ: float32 [2048], P('orb'), may hold values from 0.1 to 2
- v_loc: float32 [49152], P('dom'), may hold values from -1 to 1
Outputs:
- rotated: float32 [49152, 2048], P('dom', 'orb')
- density: float32 [49152], P('dom')
- hpsi: float32 [49152, 2048], P('dom', 'orb')
- band: float32 [2048], P('orb')
The draws below stay inside these ranges and needn't reach their ends.
All inputs are finite; a program needn't handle non-finite values.
Results may differ from the reference program's by a relative error of at most 0.000075.
Values sent between devices are 32-bit elements; how exact they have to be, the bound alone decides.
A program may use at most 128 MiB of HBM per device.

```python
import math
import jax
import jax.numpy as jnp
from jax import lax

M = 2048
NY = 8
NZ = 128
NX = 48
NPTS = 49152


def levels(rng, dims, pieces, low, high):
    gain, own = 1.0, jax.random.fold_in(rng, 6)
    for dim, shards_of in pieces:
        draws = jnp.exp(jax.random.uniform(jax.random.fold_in(own, dim), (shards_of,), jnp.float32, low / len(pieces), high / len(pieces)))
        gain = gain * jnp.repeat(draws, dims[dim] // shards_of).reshape([-1 if axis == dim else 1 for axis in range(len(dims))])
    return gain


def gaussian(key, shape, deviation, reach, split=(), kind=jnp.bfloat16):
    values = jax.random.normal(key, shape, jnp.float32) * deviation
    if len(split) > 0:
        values = levels(key, shape, split, -0.22, 0.18) * values
    return jnp.clip(values, min=-reach, max=reach).astype(kind)


def setup_inputs(seed: int = 0) -> dict:
    keys = jax.random.split(jax.random.key(seed), 5)
    return {
        "psi": gaussian(keys[0], (NPTS, M), 1.0, 6.0, ((0, 16), (1, 16)), jnp.float32),
        "rot": gaussian(keys[1], (M, M), M ** -0.5, 0.125, ((1, 16),), jnp.float32),
        "occ": jnp.clip(jnp.exp(math.log(2.0) - 2.9957323 * jax.random.uniform(keys[2], (M,), jnp.float32) ** levels(keys[2], (M,), ((0, 16),), -0.2, 0.2)), 0.1, 2.0),
        "v_loc": jnp.clip(jax.random.uniform(keys[3], (NPTS,), jnp.float32, -1.0, 1.0) * levels(keys[3], (NPTS,), ((0, 16),), -0.4, 0.0), -1.0, 1.0),
    }


def reference(psi, rot, occ, v_loc):
    rotated = jnp.dot(psi, rot, precision=lax.Precision.HIGHEST, preferred_element_type=jnp.float32)
    density = jnp.sum(occ[None, :] * rotated * rotated, axis=1) / M
    potential = v_loc - (3.0 / jnp.pi) ** (1.0 / 3.0) * jnp.cbrt(density)
    field = rotated.reshape(NX, NY, NZ, M)
    beside = jnp.roll(field, 1, 0) + jnp.roll(field, -1, 0)
    beside = beside + jnp.roll(field, 1, 1) + jnp.roll(field, -1, 1)
    beside = beside + jnp.roll(field, 1, 2) + jnp.roll(field, -1, 2)
    lap = (beside - 6.0 * field).reshape(NPTS, M)
    hpsi = -0.5 * lap + potential[:, None] * rotated
    band = jnp.sum(rotated * hpsi, axis=0) / NPTS
    return rotated, density, hpsi, band
```

```python
import functools

import jax
import jax.numpy as jnp
from jax import lax
from jax.experimental import pallas as pl
from jax.experimental.pallas import tpu as pltpu
from jax.sharding import PartitionSpec as P

M = 2048
PTS = 3072
NORB = 128
NLINE = 24
LINE = 128
NPTS = 49152
AHEAD = 3
LAG_C = 2
LAG_D = 4
LAG_E = 6
MESH = pl.DeviceIdType.MESH
HIGHEST = lax.Precision.HIGHEST


def line_of(k):
    q = k // 8
    return (2 * q - 3 * (q // 2)) * 8 + k % 8


def split(v):
    hi = v.astype(jnp.bfloat16)
    return hi, (v - hi.astype(jnp.float32)).astype(jnp.bfloat16)


def cbrt(d):
    safe = jnp.maximum(d, 1e-37)
    y = jnp.exp(jnp.log(safe) * (1.0 / 3.0))
    y = y - (y - safe / (y * y)) * (1.0 / 3.0)
    return jnp.where(d < 1e-37, 0.0, y)


def kernel(psi, rot, occ, vloc, rotated, dens, hpsi, band,
           abuf, rotv, rbuf, bhi, blo, part, rsb, halo, dpart, dx, dsum, dz, bpart, b1, bsum, b2,
           in_sem, a_recv, a_send, rs_recv, rs_send, h_recv, h_send, r1_sem, r2_send, r2_recv,
           d_send, d_recv, b_send, b_recv):
    dom = lax.axis_index("dom")
    orb = lax.axis_index("orb")
    y, zh, c = dom // 4, (dom // 2) % 2, dom % 2
    z, x = orb // 4, orb % 4
    z1, z0 = z // 2, z % 2
    xp, xm, xo = (x + 1) % 4, (x + 3) % 4, (x + 2) % 4
    at_xp, at_xm = (dom, z * 4 + xp), (dom, z * 4 + xm)
    at_z0 = (dom, (z1 * 2 + 1 - z0) * 4 + x)
    at_z1 = (dom, ((1 - z1) * 2 + z0) * 4 + x)
    at_prev, at_next = ((dom + 15) % 16, orb), ((dom + 1) % 16, orb)
    e = y * 2 + c

    def at_yc(f):
        return ((f // 2) * 4 + zh * 2 + f % 2, orb)

    x_peers = [(dom, z * 4 + (x + j) % 4) for j in (1, 2, 3)]
    z_peers = [(dom, ((z + j) % 4) * 4 + x) for j in (1, 2, 3)]
    yc_peers = [at_yc((e + j) % 8) for j in range(1, 8)]
    s = zh * 2 + c
    zc_peers = [(y * 4 + (s + j) % 4, orb) for j in (1, 2, 3)]
    y_peers = [(((y + j) % 4) * 4 + s, orb) for j in (1, 2, 3)]

    own, pb = z0 * 4 + x, (1 - z0) * 4 + x
    load_psi = pltpu.make_async_copy(psi, abuf.at[own], in_sem.at[0])
    load_psi.start()
    load_rot = pltpu.make_async_copy(rot, rotv, in_sem.at[1])
    load_rot.start()

    barrier = pltpu.get_barrier_semaphore()
    everyone = x_peers + z_peers + yc_peers + zc_peers + [at_prev, at_next]
    for peer in everyone:
        pl.semaphore_signal(barrier, inc=1, device_id=peer, device_id_type=MESH)
    pl.semaphore_wait(barrier, len(everyone))
    load_psi.wait()
    load_rot.wait()

    def remote(src, dst, send, recv, peer):
        return pltpu.make_async_remote_copy(
            src_ref=src, dst_ref=dst, send_sem=send, recv_sem=recv, device_id=peer, device_id_type=MESH)

    def rows_of(k):
        return pl.ds(pl.multiple_of(line_of(k) * LINE, LINE), LINE)

    def block(b, k, way, peer):
        ref = abuf.at[b, rows_of(k)]
        return remote(ref, ref, a_send.at[way], a_recv.at[b, k], peer)

    def got(b, k):
        block(b, k, 0, at_xp).wait_recv()

    def send_own(k):
        block(own, k, 0, at_z0).start()
        block(own, k, 1, at_xp).start()
        block(own, k, 2, at_xm).start()

    send_r1 = remote(
        rotv.at[pl.ds(pl.multiple_of((1 - z1) * 1024 + e * 128, 128), 128)], rbuf.at[e],
        r1_sem.at[0], r1_sem.at[1], at_z1)
    send_r1.start()
    for k in range(AHEAD):
        send_own(k)

    def share(j):
        return remote(rbuf.at[e], rbuf.at[e], r2_send.at[j], r2_recv.at[e], yc_peers[j])

    def rs_copy(k):
        rows = rows_of(k)
        return remote(part.at[rows], rsb.at[rows], rs_send.at[0], rs_recv.at[k], at_z1)

    def step(i, _):
        @pl.when(i + AHEAD < NLINE)
        def _():
            send_own(i + AHEAD)

        @pl.when(i < NLINE)
        def _():
            got(pb, i)
            block(pb, i, 3, at_xp).start()
            block(pb, i, 4, at_xm).start()
            got(z0 * 4 + xm, i)
            block(z0 * 4 + xm, i, 5, at_xp).start()

        @pl.when(i == 0)
        def _():
            send_r1.wait_recv()
            for j in range(7):
                share(j).start()

        @pl.when((i >= LAG_C) & (i < NLINE + LAG_C))
        def _():
            k = i - LAG_C
            got((1 - z0) * 4 + xp, k)
            block((1 - z0) * 4 + xp, k, 6, at_xm).start()

        @pl.when(i == LAG_D)
        def _():
            for j in range(1, 8):
                f = (e + j) % 8
                remote(rbuf.at[f], rbuf.at[f], r2_send.at[0], r2_recv.at[f], at_z1).wait_recv()
            hi, lo = split(rotv[pl.ds(pl.multiple_of(z1 * 1024, 1024), 1024), :])
            bhi[:, :NORB] = hi
            blo[:, :NORB] = lo
            hi, lo = split(rbuf[...].reshape(1024, NORB))
            bhi[:, NORB:] = hi
            blo[:, NORB:] = lo

        @pl.when((i >= LAG_D) & (i < NLINE + LAG_D))
        def _():
            k = i - LAG_D
            got((1 - z0) * 4 + xm, k)
            got(z0 * 4 + xp, k)
            got(z0 * 4 + xo, k)
            got((1 - z0) * 4 + xo, k)
            rows = rows_of(k)
            a = jnp.concatenate([abuf[b, rows, :] for b in range(8)], axis=1)
            hi, lo = split(a)
            total = jnp.dot(hi, blo[...], preferred_element_type=jnp.float32)
            total += jnp.dot(lo, bhi[...], preferred_element_type=jnp.float32)
            total += jnp.dot(hi, bhi[...], preferred_element_type=jnp.float32)
            rotated[rows, :] = total[:, :NORB]
            part[rows, :] = total[:, NORB:]

        @pl.when((i >= LAG_E + 1) & (i < 16 + LAG_E + 1))
        def _():
            k = i - LAG_E - 1
            rows = rows_of(k)
            there = pl.ds(pl.multiple_of((k % 8) * LINE, LINE), LINE)

            @pl.when(k < 8)
            def _():
                remote(rotated.at[rows], halo.at[1, there], h_send.at[0], h_recv.at[1], at_prev).start()

            @pl.when(k >= 8)
            def _():
                remote(rotated.at[rows], halo.at[0, there], h_send.at[1], h_recv.at[0], at_next).start()

        @pl.when((i >= LAG_E) & (i < NLINE + LAG_E))
        def _():
            k = i - LAG_E
            rs_copy(k).wait_recv()
            rows = rows_of(k)
            r = rotated[rows, :] + rsb[rows, :]
            rotated[rows, :] = r
            d = lax.dot_general(jnp.broadcast_to(occ[...], (8, NORB)), r * r, (((1,), (1,)), ((), ())),
                                precision=HIGHEST, preferred_element_type=jnp.float32)
            dpart[pl.ds(line_of(k), 1), :] = d[0:1]

        @pl.when((i >= LAG_D) & (i < NLINE + LAG_D))
        def _():
            rs_copy(i - LAG_D).start()

        return 0

    lax.fori_loop(0, NLINE + LAG_E, step, 0)

    for way, peer in enumerate([at_z0, at_xp, at_xm, at_xp, at_xm, at_xp, at_xm]):
        remote(abuf.at[own], abuf.at[own], a_send.at[way], a_recv.at[0, 0], peer).wait_send()

    def exchange(src, dst, send, recv, base, peers):
        return [remote(src, dst.at[2 - j], send.at[base + j], recv.at[base + 2 - j], peer)
                for j, peer in enumerate(peers)]

    stage = exchange(dpart, dx, d_send, d_recv, 0, x_peers)
    for copy in stage:
        copy.start()

    remote(halo.at[0], halo.at[0], h_send.at[0], h_recv.at[0], at_next).wait_recv()
    remote(halo.at[1], halo.at[1], h_send.at[0], h_recv.at[1], at_next).wait_recv()

    def beside_line(p, line):
        rows = pl.ds(line * LINE, LINE)
        r = rotated[pl.ds((p * 8 + line) * LINE, LINE), :]
        below = rotated[pl.ds(((p - 1) * 8 + line) * LINE, LINE), :] if p > 0 else halo[0, rows, :]
        above = rotated[pl.ds(((p + 1) * 8 + line) * LINE, LINE), :] if p < 2 else halo[1, rows, :]
        total = below + above
        total += rotated[pl.ds((p * 8 + (line + 1) % 8) * LINE, LINE), :]
        total += rotated[pl.ds((p * 8 + (line + 7) % 8) * LINE, LINE), :]
        total += pltpu.roll(r, 1, 0) + pltpu.roll(r, LINE - 1, 0)
        return r, 3.0 * r - 0.5 * total

    acc = jnp.zeros((8, NORB), jnp.float32)
    for p in range(3):
        for line in range(8):
            r, h = beside_line(p, line)
            hpsi[pl.ds((p * 8 + line) * LINE, LINE), :] = h
            acc += jnp.sum((r * h).reshape(LINE // 8, 8, NORB), axis=0)

    for copy in stage:
        copy.wait_recv()
    dsum[...] = dpart[...] + dx[0] + dx[1] + dx[2]
    for copy in stage:
        copy.wait_send()
    stage = exchange(dsum, dz, d_send, d_recv, 3, z_peers)
    for copy in stage:
        copy.start()
    for copy in stage:
        copy.wait_recv()
    density = (dsum[...] + dz[0] + dz[1] + dz[2]) * (1.0 / M)
    for copy in stage:
        copy.wait_send()
    dens[...] = density
    pot = vloc[...] - (3.0 / jnp.pi) ** (1.0 / 3.0) * cbrt(density)

    extra = jnp.zeros((8, NORB), jnp.float32)
    for n in range(NLINE):
        r = rotated[pl.ds(n * LINE, LINE), :]
        extra += jnp.dot(jnp.broadcast_to(pot[n:n + 1], (8, LINE)), r * r,
                         precision=HIGHEST, preferred_element_type=jnp.float32)
    mine = jnp.sum(acc, axis=0, keepdims=True) + extra[0:1]
    bpart[...] = jnp.broadcast_to(mine, (8, NORB))
    stage = exchange(bpart, b1, b_send, b_recv, 0, zc_peers)
    for copy in stage:
        copy.start()

    for n in range(NLINE):
        rows = pl.ds(n * LINE, LINE)
        column = jnp.broadcast_to(pot[n:n + 1], (LINE, LINE)).T
        hpsi[rows, :] = hpsi[rows, :] + column * rotated[rows, :]

    for copy in stage:
        copy.wait_recv()
    bsum[...] = bpart[...] + b1[0] + b1[1] + b1[2]
    for copy in stage:
        copy.wait_send()
    stage = exchange(bsum, b2, b_send, b_recv, 3, y_peers)
    for copy in stage:
        copy.start()
    for copy in stage:
        copy.wait_recv()
    band[...] = ((bsum[...] + b2[0] + b2[1] + b2[2]) * (1.0 / NPTS))[0:1]
    for copy in stage:
        copy.wait_send()

    send_r1.wait_send()
    for j in range(7):
        share(j).wait_send()
    whole = pl.ds(0, PTS)
    remote(part.at[whole], rsb.at[whole], rs_send.at[0], rs_recv.at[0], at_z1).wait_send()
    for side in range(2):
        remote(halo.at[0], halo.at[0], h_send.at[side], h_recv.at[0], at_next).wait_send()


def shards(psi, rot, occ, v_loc):
    f32 = jnp.float32
    vmem, hbm = pl.BlockSpec(memory_space=pltpu.VMEM), pl.BlockSpec(memory_space=pl.ANY)
    dma = pltpu.SemaphoreType.DMA
    rotated, density, hpsi, band = pl.pallas_call(
        kernel,
        out_shape=(
            jax.ShapeDtypeStruct((PTS, NORB), f32),
            jax.ShapeDtypeStruct((NLINE, LINE), f32),
            jax.ShapeDtypeStruct((PTS, NORB), f32),
            jax.ShapeDtypeStruct((1, NORB), f32),
        ),
        in_specs=[hbm, hbm, vmem, vmem],
        out_specs=(vmem, vmem, vmem, vmem),
        scratch_shapes=[
            pltpu.VMEM((8, PTS, NORB), f32),
            pltpu.VMEM((M, NORB), f32),
            pltpu.VMEM((8, 128, NORB), f32),
            pltpu.VMEM((1024, 2 * NORB), jnp.bfloat16),
            pltpu.VMEM((1024, 2 * NORB), jnp.bfloat16),
            pltpu.VMEM((PTS, NORB), f32),
            pltpu.VMEM((PTS, NORB), f32),
            pltpu.VMEM((2, 1024, NORB), f32),
            pltpu.VMEM((NLINE, LINE), f32),
            pltpu.VMEM((3, NLINE, LINE), f32),
            pltpu.VMEM((NLINE, LINE), f32),
            pltpu.VMEM((3, NLINE, LINE), f32),
            pltpu.VMEM((8, NORB), f32),
            pltpu.VMEM((3, 8, NORB), f32),
            pltpu.VMEM((8, NORB), f32),
            pltpu.VMEM((3, 8, NORB), f32),
            dma((2,)),
            dma((8, NLINE)),
            dma((7,)),
            dma((NLINE,)),
            dma((1,)),
            dma((2,)),
            dma((2,)),
            dma((2,)),
            dma((7,)),
            dma((8,)),
            dma((6,)),
            dma((6,)),
            dma((6,)),
            dma((6,)),
        ],
        compiler_params=pltpu.CompilerParams(
            collective_id=0, has_side_effects=True, vmem_limit_bytes=56 * 1024 * 1024),
        name="rotate",
    )(psi, rot, occ.reshape(1, NORB), v_loc.reshape(NLINE, LINE))
    return rotated, density.reshape(PTS), hpsi, band.reshape(NORB)


def solution(mesh):
    placed = (P("dom", "orb"), P(None, "orb"), P("orb"), P("dom"))
    return jax.shard_map(
        shards,
        mesh=mesh,
        in_specs=placed,
        out_specs=(P("dom", "orb"), P("dom"), P("dom", "orb"), P("orb")),
        check_vma=False,
    )
```

```python
import functools

import jax
import jax.numpy as jnp
from jax import lax
from jax.experimental import pallas as pl
from jax.experimental.pallas import tpu as pltpu
from jax.sharding import PartitionSpec as P

M = 2048
PTS = 3072
NORB = 128
NLINE = 24
LINE = 128
NPTS = 49152
AHEAD = 3
LAG_C = 1
LAG_D = 2
LAG_E = 4
MESH = pl.DeviceIdType.MESH
HIGHEST = lax.Precision.HIGHEST


def line_of(k):
    q = k // 8
    return (2 * q - 3 * (q // 2)) * 8 + k % 8


def split(v):
    hi = v.astype(jnp.bfloat16)
    return hi, (v - hi.astype(jnp.float32)).astype(jnp.bfloat16)


def cbrt(d):
    safe = jnp.maximum(d, 1e-37)
    y = jnp.exp(jnp.log(safe) * (1.0 / 3.0))
    y = y - (y - safe / (y * y)) * (1.0 / 3.0)
    return jnp.where(d < 1e-37, 0.0, y)


def kernel(psi, rot, occ_hbm, vloc_hbm, rotated, dens, hpsi, band,
           occ, vloc, abuf, rotv, rbuf, bhi, blo, part, rsb, halo, dpart, dxa, dxb, bpart, bx,
           in_sem, a_recv, a_send, rs_recv, rs_send, h_recv, h_send, r1_sem, r2_send, r2_recv,
           d_send, d_recv, b_send, b_recv):
    dom = lax.axis_index("dom")
    orb = lax.axis_index("orb")
    y, zh, c = dom // 4, (dom // 2) % 2, dom % 2
    z, x = orb // 4, orb % 4
    z1, z0 = z // 2, z % 2
    xp, xm, xo = (x + 1) % 4, (x + 3) % 4, (x + 2) % 4
    at_xp, at_xm = (dom, z * 4 + xp), (dom, z * 4 + xm)
    at_z0 = (dom, (z1 * 2 + 1 - z0) * 4 + x)
    at_z1 = (dom, ((1 - z1) * 2 + z0) * 4 + x)
    at_prev, at_next = ((dom + 15) % 16, orb), ((dom + 1) % 16, orb)
    e = y * 2 + c

    def at_yc(f):
        return ((f // 2) * 4 + zh * 2 + f % 2, orb)

    orb_peers = [(dom, (orb + j) % 16) for j in range(1, 16)]
    dom_peers = [((dom + j) % 16, orb) for j in range(1, 16)]
    yc_peers = [at_yc((e + j) % 8) for j in range(1, 8)]

    own, pb = z0 * 4 + x, (1 - z0) * 4 + x
    loads = [pltpu.make_async_copy(src, dst, in_sem.at[n]) for n, (src, dst) in enumerate(
        [(psi, abuf.at[own]), (rot, rotv), (occ_hbm, occ), (vloc_hbm, vloc)])]
    for load in loads:
        load.start()

    barrier = pltpu.get_barrier_semaphore()
    everyone = orb_peers + dom_peers
    for peer in everyone:
        pl.semaphore_signal(barrier, inc=1, device_id=peer, device_id_type=MESH)
    pl.semaphore_wait(barrier, len(everyone))
    for load in loads:
        load.wait()

    def remote(src, dst, send, recv, peer):
        return pltpu.make_async_remote_copy(
            src_ref=src, dst_ref=dst, send_sem=send, recv_sem=recv, device_id=peer, device_id_type=MESH)

    def rows_of(k):
        return pl.ds(pl.multiple_of(line_of(k) * LINE, LINE), LINE)

    def block(b, k, way, peer):
        ref = abuf.at[b, rows_of(k)]
        return remote(ref, ref, a_send.at[way], a_recv.at[b, k], peer)

    def got(b, k):
        block(b, k, 0, at_xp).wait_recv()

    def send_own(k):
        block(own, k, 0, at_z0).start()
        block(own, k, 1, at_xp).start()
        block(own, k, 2, at_xm).start()

    send_r1 = remote(
        rotv.at[pl.ds(pl.multiple_of((1 - z1) * 1024 + e * 128, 128), 128)], rbuf.at[e],
        r1_sem.at[0], r1_sem.at[1], at_z1)
    send_r1.start()
    for k in range(AHEAD):
        send_own(k)

    def share(j):
        return remote(rbuf.at[e], rbuf.at[e], r2_send.at[j], r2_recv.at[e], yc_peers[j])

    def rs_copy(k):
        rows = rows_of(k)
        return remote(part.at[rows], rsb.at[rows], rs_send.at[0], rs_recv.at[k], at_z1)

    def to_all(src, dst, send, recv, peers):
        for j, peer in enumerate(peers):
            remote(src, dst.at[14 - j], send, recv, peer).start()

    def from_all(dst, send, recv, peers):
        return remote(dst, dst, send, recv, peers[0])

    def step(i, _):
        @pl.when(i + AHEAD < NLINE)
        def _():
            send_own(i + AHEAD)

        @pl.when(i < NLINE)
        def _():
            got(pb, i)
            block(pb, i, 3, at_xp).start()
            block(pb, i, 4, at_xm).start()
            got(z0 * 4 + xm, i)
            block(z0 * 4 + xm, i, 5, at_xp).start()

        @pl.when(i == 0)
        def _():
            send_r1.wait_recv()
            for j in range(7):
                share(j).start()

        @pl.when((i >= LAG_C) & (i < NLINE + LAG_C))
        def _():
            k = i - LAG_C
            got((1 - z0) * 4 + xp, k)
            block((1 - z0) * 4 + xp, k, 6, at_xm).start()

        @pl.when(i == LAG_D)
        def _():
            for j in range(1, 8):
                f = (e + j) % 8
                remote(rbuf.at[f], rbuf.at[f], r2_send.at[0], r2_recv.at[f], at_z1).wait_recv()
            hi, lo = split(rotv[pl.ds(pl.multiple_of(z1 * 1024, 1024), 1024), :])
            bhi[:, :NORB] = hi
            blo[:, :NORB] = lo
            hi, lo = split(rbuf[...].reshape(1024, NORB))
            bhi[:, NORB:] = hi
            blo[:, NORB:] = lo

        @pl.when((i >= LAG_D) & (i < NLINE + LAG_D))
        def _():
            k = i - LAG_D
            got((1 - z0) * 4 + xm, k)
            got(z0 * 4 + xp, k)
            got(z0 * 4 + xo, k)
            got((1 - z0) * 4 + xo, k)
            rows = rows_of(k)
            a = jnp.concatenate([abuf[b, rows, :] for b in range(8)], axis=1)
            hi, lo = split(a)
            total = jnp.dot(hi, blo[...], preferred_element_type=jnp.float32)
            total += jnp.dot(lo, bhi[...], preferred_element_type=jnp.float32)
            total += jnp.dot(hi, bhi[...], preferred_element_type=jnp.float32)
            rotated[rows, :] = total[:, :NORB]
            part[rows, :] = total[:, NORB:]

        @pl.when((i >= LAG_E + 1) & (i < 16 + LAG_E + 1))
        def _():
            k = i - LAG_E - 1
            rows = rows_of(k)
            there = pl.ds(pl.multiple_of((k % 8) * LINE, LINE), LINE)

            @pl.when(k < 8)
            def _():
                remote(rotated.at[rows], halo.at[1, there], h_send.at[0], h_recv.at[1], at_prev).start()

            @pl.when(k >= 8)
            def _():
                remote(rotated.at[rows], halo.at[0, there], h_send.at[1], h_recv.at[0], at_next).start()

        @pl.when((i >= LAG_E) & (i < NLINE + LAG_E))
        def _():
            k = i - LAG_E
            rs_copy(k).wait_recv()
            rows = rows_of(k)
            r = rotated[rows, :] + rsb[rows, :]
            rotated[rows, :] = r
            d = lax.dot_general(jnp.broadcast_to(occ[...], (8, NORB)), r * r, (((1,), (1,)), ((), ())),
                                precision=HIGHEST, preferred_element_type=jnp.float32)
            dpart[pl.ds(k, 1), :] = d[0:1]

        @pl.when((i >= LAG_D) & (i < NLINE + LAG_D))
        def _():
            rs_copy(i - LAG_D).start()

        @pl.when(i == LAG_E + 17)
        def _():
            to_all(dpart.at[pl.ds(0, 16)], dxa, d_send.at[0], d_recv.at[0], orb_peers)

        return 0

    lax.fori_loop(0, NLINE + LAG_E, step, 0)

    for way, peer in enumerate([at_z0, at_xp, at_xm, at_xp, at_xm, at_xp, at_xm]):
        remote(abuf.at[own], abuf.at[own], a_send.at[way], a_recv.at[0, 0], peer).wait_send()

    to_all(dpart.at[pl.ds(16, 8)], dxb, d_send.at[1], d_recv.at[1], orb_peers)

    remote(halo.at[0], halo.at[0], h_send.at[0], h_recv.at[0], at_next).wait_recv()
    remote(halo.at[1], halo.at[1], h_send.at[0], h_recv.at[1], at_next).wait_recv()

    for p in range(3):
        for line in range(8):
            rows = pl.ds(line * LINE, LINE)
            here = pl.ds((p * 8 + line) * LINE, LINE)
            r = rotated[here, :]
            total = rotated[pl.ds(((p - 1) * 8 + line) * LINE, LINE), :] if p > 0 else halo[0, rows, :]
            total += rotated[pl.ds(((p + 1) * 8 + line) * LINE, LINE), :] if p < 2 else halo[1, rows, :]
            total += rotated[pl.ds((p * 8 + (line + 1) % 8) * LINE, LINE), :]
            total += rotated[pl.ds((p * 8 + (line + 7) % 8) * LINE, LINE), :]
            total += pltpu.roll(r, 1, 0) + pltpu.roll(r, LINE - 1, 0)
            hpsi[here, :] = 3.0 * r - 0.5 * total

    from_all(dxa, d_send.at[0], d_recv.at[0], orb_peers).wait_recv()
    from_all(dxb, d_send.at[1], d_recv.at[1], orb_peers).wait_recv()
    first, last = dpart[0:16], dpart[16:24]
    for j in range(15):
        first += dxa[j]
        last += dxb[j]
    density = jnp.concatenate([first[0:8], last, first[8:16]], axis=0) * (1.0 / M)
    dens[...] = density
    pot = vloc[...] - (3.0 / jnp.pi) ** (1.0 / 3.0) * cbrt(density)
    turned = jnp.concatenate([pot, jnp.zeros((LINE - NLINE, LINE), jnp.float32)], axis=0).T

    acc = jnp.zeros((8, NORB), jnp.float32)
    for n in range(NLINE):
        rows = pl.ds(n * LINE, LINE)
        r = rotated[rows, :]
        h = hpsi[rows, :] + jnp.broadcast_to(turned[:, n:n + 1], (LINE, NORB)) * r
        hpsi[rows, :] = h
        acc += jnp.sum((r * h).reshape(LINE // 8, 8, NORB), axis=0)
    bpart[...] = acc
    from_all(dxa, d_send.at[0], d_recv.at[0], orb_peers).wait_send()
    from_all(dxb, d_send.at[1], d_recv.at[1], orb_peers).wait_send()
    to_all(bpart, bx, b_send.at[0], b_recv.at[0], dom_peers)
    shared = from_all(bx, b_send.at[0], b_recv.at[0], dom_peers)
    shared.wait_recv()
    total = acc
    for j in range(15):
        total += bx[j]
    band[...] = jnp.sum(total, axis=0, keepdims=True) * (1.0 / NPTS)
    shared.wait_send()

    send_r1.wait_send()
    for j in range(7):
        share(j).wait_send()
    whole = pl.ds(0, PTS)
    remote(part.at[whole], rsb.at[whole], rs_send.at[0], rs_recv.at[0], at_z1).wait_send()
    for side in range(2):
        remote(halo.at[0], halo.at[0], h_send.at[side], h_recv.at[0], at_next).wait_send()


def put_kernel(*refs):
    count = len(refs) // 2
    sem = refs[-1]
    copies = [pltpu.make_async_copy(refs[n], refs[count + n], sem.at[n]) for n in range(count)]
    for copy in copies:
        copy.start()
    for copy in copies:
        copy.wait()


def put(*arrays):
    hbm = pl.BlockSpec(memory_space=pl.ANY)
    return pl.pallas_call(
        put_kernel,
        out_shape=tuple(jax.ShapeDtypeStruct(a.shape, a.dtype) for a in arrays),
        in_specs=[hbm] * len(arrays),
        out_specs=(hbm,) * len(arrays),
        scratch_shapes=[pltpu.SemaphoreType.DMA((len(arrays),))],
        compiler_params=pltpu.CompilerParams(vmem_limit_bytes=16 * 1024 * 1024),
        name="put",
    )(*arrays)


def shards(psi, rot, occ, v_loc):
    f32 = jnp.float32
    vmem, hbm = pl.BlockSpec(memory_space=pltpu.VMEM), pl.BlockSpec(memory_space=pltpu.HBM)
    dma = pltpu.SemaphoreType.DMA
    rotated, density, hpsi, band = pl.pallas_call(
        kernel,
        out_shape=(
            jax.ShapeDtypeStruct((PTS, NORB), f32),
            jax.ShapeDtypeStruct((NLINE, LINE), f32),
            jax.ShapeDtypeStruct((PTS, NORB), f32),
            jax.ShapeDtypeStruct((1, NORB), f32),
        ),
        in_specs=[hbm] * 4,
        out_specs=(vmem, vmem, vmem, vmem),
        scratch_shapes=[
            pltpu.VMEM((1, NORB), f32),
            pltpu.VMEM((NLINE, LINE), f32),
            pltpu.VMEM((8, PTS, NORB), f32),
            pltpu.VMEM((M, NORB), f32),
            pltpu.VMEM((8, 128, NORB), f32),
            pltpu.VMEM((1024, 2 * NORB), jnp.bfloat16),
            pltpu.VMEM((1024, 2 * NORB), jnp.bfloat16),
            pltpu.VMEM((PTS, NORB), f32),
            pltpu.VMEM((PTS, NORB), f32),
            pltpu.VMEM((2, 1024, NORB), f32),
            pltpu.VMEM((NLINE, LINE), f32),
            pltpu.VMEM((15, 16, LINE), f32),
            pltpu.VMEM((15, 8, LINE), f32),
            pltpu.VMEM((8, NORB), f32),
            pltpu.VMEM((15, 8, NORB), f32),
            dma((4,)),
            dma((8, NLINE)),
            dma((7,)),
            dma((NLINE,)),
            dma((1,)),
            dma((2,)),
            dma((2,)),
            dma((2,)),
            dma((7,)),
            dma((8,)),
            dma((2,)),
            dma((2,)),
            dma((1,)),
            dma((1,)),
        ],
        compiler_params=pltpu.CompilerParams(
            collective_id=0, has_side_effects=True, vmem_limit_bytes=40 * 1024 * 1024),
        name="rotate",
    )(*[pltpu.with_memory_space_constraint(v, pltpu.HBM) for v in (
        psi, rot, occ.reshape(1, NORB), v_loc.reshape(NLINE, LINE))])
    return put(rotated, density.reshape(PTS), hpsi, band.reshape(NORB))


def solution(mesh):
    placed = (P("dom", "orb"), P(None, "orb"), P("orb"), P("dom"))
    return jax.shard_map(
        shards,
        mesh=mesh,
        in_specs=placed,
        out_specs=(P("dom", "orb"), P("dom"), P("dom", "orb"), P("orb")),
        check_vma=False,
    )
```

```python
import functools

import jax
import jax.numpy as jnp
from jax import lax
from jax.experimental import pallas as pl
from jax.experimental.pallas import tpu as pltpu
from jax.sharding import PartitionSpec as P

M = 2048
PTS = 3072
NORB = 128
NLINE = 24
LINE = 128
NPTS = 49152
N = 12
HALF = N * LINE
AHEAD1 = 3
AHEAD2 = 4
LAG_1 = 2
HOP = 1
DONE_1 = LAG_1 + 3 * HOP
LAG_2 = 3
DONE_2 = 4
MESH = pl.DeviceIdType.MESH
HIGHEST = lax.Precision.HIGHEST


def line_2(k):
    return k + 16 - 12 * (k // 8)


def split(v):
    hi = v.astype(jnp.bfloat16)
    return hi, (v - hi.astype(jnp.float32)).astype(jnp.bfloat16)


def cbrt(d):
    safe = jnp.maximum(d, 1e-37)
    y = jnp.exp(jnp.log(safe) * (1.0 / 3.0))
    y = y - (y - safe / (y * y)) * (1.0 / 3.0)
    return jnp.where(d < 1e-37, 0.0, y)


def kernel(psi, rot, occ_hbm, vloc_hbm, rotated, dens, hpsi, band,
           occ, vloc, a1, a2, rotv, rb1, rb2, b1hi, b1lo, b2hi, b2lo, q, into_r, into_l, p2, rs2, halo, dpart, dx, bpart, bx,
           in_sem, a1_recv, a1_send, a2_recv, a2_send, r1_send, r1_recv, s1_send, s1_recv, r2_send, r2_recv, s2_sem,
           r_recv, r_send, l_recv, l_send, rs_recv, rs_send, h_recv, h_send, d_send, d_recv, b_send, b_recv):
    dom = lax.axis_index("dom")
    orb = lax.axis_index("orb")
    y, zh, c = dom // 4, (dom // 2) % 2, dom % 2
    z, x = orb // 4, orb % 4
    at_right, at_left = (dom, ((z + 1) % 4) * 4 + x), (dom, ((z + 3) % 4) * 4 + x)
    at_prev, at_next = ((dom + 15) % 16, orb), ((dom + 1) % 16, orb)
    at_twin = (dom + 1 - 2 * c, orb)
    e = y * 2 + c

    def at_yc(f):
        return ((f // 2) * 4 + zh * 2 + f % 2, orb)

    x_peers = [(dom, z * 4 + (x + j) % 4) for j in (1, 2, 3)]
    z_peers = [(dom, ((z + j) % 4) * 4 + x) for j in (1, 2, 3)]
    orb_peers = [(dom, (orb + j) % 16) for j in range(1, 16)]
    dom_peers = [((dom + j) % 16, orb) for j in range(1, 16)]
    yc_peers = [at_yc((e + j) % 8) for j in range(1, 8)]

    loads = [pltpu.make_async_copy(src, dst, in_sem.at[n]) for n, (src, dst) in enumerate([
        (psi.at[pl.ds(0, HALF)], a1.at[x]),
        (psi.at[pl.ds(2048, 1024)], a2.at[z, pl.ds(0, 1024)]),
        (psi.at[pl.ds(HALF, 512)], a2.at[z, pl.ds(1024, 512)]),
        (rot, rotv), (occ_hbm, occ), (vloc_hbm, vloc)])]
    for load in loads:
        load.start()

    barrier = pltpu.get_barrier_semaphore()
    everyone = orb_peers + dom_peers
    for peer in everyone:
        pl.semaphore_signal(barrier, inc=1, device_id=peer, device_id_type=MESH)
    pl.semaphore_wait(barrier, len(everyone))
    for load in loads:
        load.wait()

    def remote(src, dst, send, recv, peer):
        return pltpu.make_async_remote_copy(
            src_ref=src, dst_ref=dst, send_sem=send, recv_sem=recv, device_id=peer, device_id_type=MESH)

    def at(n, size):
        return pl.ds(pl.multiple_of(n * size, size), size)

    def send_1(k):
        ref = a1.at[x, at(k, LINE)]
        for j in range(3):
            remote(ref, ref, a1_send.at[j], a1_recv.at[x, k], x_peers[j]).start()

    def block_2(b, k, way):
        ref = a2.at[b, at(k, LINE)]
        return remote(ref, ref, a2_send.at[way, b], a2_recv.at[b, k], at_left if way else at_right)

    def got_2(b, k):
        block_2(b, k, 0).wait_recv()

    def send_2(k):
        @pl.when(z < 3)
        def _():
            block_2(z, k, 0).start()

        @pl.when(z > 0)
        def _():
            block_2(z, k, 1).start()

    def rot_1(j):
        return remote(rotv.at[at(((z + j + 1) % 4) * 8 + e, 64)], rb1.at[e, 2 - j],
                      r1_send.at[j], r1_recv.at[2 - j], z_peers[j])

    def share_1(j):
        return remote(rb1.at[e], rb1.at[e], s1_send.at[j], s1_recv.at[e], yc_peers[j])

    def rot_2(j, n):
        return remote(rotv.at[at((2 * c + n) * 4 + (x + j + 1) % 4, 128)], rb2.at[c, 2 - j, n],
                      r2_send.at[j, n], r2_recv.at[2 - j, n], x_peers[j])

    share_2 = remote(rb2.at[c], rb2.at[c], s2_sem.at[0], s2_sem.at[1], at_twin)

    send_2(0)
    for j in range(3):
        rot_1(j).start()
    for j in range(3):
        for n in range(2):
            rot_2(j, n).start()
    for k in range(1, AHEAD2):
        send_2(k)
    for k in range(AHEAD1):
        send_1(k)

    def onward(t, k, way):
        rows = at(k, LINE)
        if way == 0:
            return remote(q.at[t, rows], into_r.at[t, rows], r_send.at[t], r_recv.at[t, k], at_right)
        return remote(q.at[t, rows], into_l.at[t, rows], l_send.at[t], l_recv.at[t, k], at_left)

    def rs_2(j, k):
        rows = at(k, LINE)
        return remote(p2.at[(x + j + 1) % 4, rows], rs2.at[2 - j, rows], rs_send.at[j], rs_recv.at[2 - j, k], x_peers[j])

    def to_all(src, dst, send, recv, peers):
        for j, peer in enumerate(peers):
            remote(src, dst.at[14 - j], send, recv, peer).start()

    def from_all(dst, send, recv, peers):
        return remote(dst, dst, send, recv, peers[0])

    def plane_sums(p):
        to_all(dpart.at[pl.ds(p * 8, 8)], dx.at[p], d_send.at[p], d_recv.at[p], orb_peers)

    def product(a, hi_ref, lo_ref):
        hi, lo = split(a)
        total = jnp.dot(hi, lo_ref[...], preferred_element_type=jnp.float32)
        total += jnp.dot(lo, hi_ref[...], preferred_element_type=jnp.float32)
        return total + jnp.dot(hi, hi_ref[...], preferred_element_type=jnp.float32)

    def finish(r, line):
        rotated[at(line, LINE), :] = r
        d = lax.dot_general(jnp.broadcast_to(occ[...], (8, NORB)), r * r, (((1,), (1,)), ((), ())),
                            precision=HIGHEST, preferred_element_type=jnp.float32)
        dpart[pl.ds(line, 1), :] = d[0:1]

    def valid(k):
        return (k >= 0) & (k < N)

    def step(i, _):
        @pl.when(i + AHEAD2 < N)
        def _():
            send_2(i + AHEAD2)

        @pl.when(i + AHEAD1 < N)
        def _():
            send_1(i + AHEAD1)

        for hop in (1, 2):
            k = i - hop + 1

            @pl.when(valid(k) & (z >= hop))
            def _(hop=hop, k=k):
                got_2(z - hop, k)

                @pl.when(z < 3)
                def _():
                    block_2(z - hop, k, 0).start()

            @pl.when(valid(k) & (z <= 3 - hop))
            def _(hop=hop, k=k):
                got_2(z + hop, k)

                @pl.when(z > 0)
                def _():
                    block_2(z + hop, k, 1).start()

        @pl.when(i == 0)
        def _():
            for j in range(3):
                rot_1(j).wait_recv()
            for j in range(7):
                share_1(j).start()

        @pl.when(i == 1)
        def _():
            for j in range(3):
                for n in range(2):
                    rot_2(j, n).wait_recv()
            share_2.start()

        @pl.when(i == LAG_2)
        def _():
            share_2.wait_recv()
            for n in range(4):
                hi, lo = split(rotv[at(n * 4 + x, 128), :])
                b2hi[pl.ds(n * 128, 128), at(x, 128)] = hi
                b2lo[pl.ds(n * 128, 128), at(x, 128)] = lo
            for j in range(3):
                hi, lo = split(rb2[:, j].reshape(512, NORB))
                b2hi[:, at((x + j + 1) % 4, 128)] = hi
                b2lo[:, at((x + j + 1) % 4, 128)] = lo

        @pl.when(i == LAG_1)
        def _():
            for j in range(1, 8):
                f = (e + j) % 8
                remote(rb1.at[f], rb1.at[f], s1_send.at[0], s1_recv.at[f], at_twin).wait_recv()
            hi, lo = split(rotv[at(z, 512), :])
            b1hi[:, at(z, 128)] = hi
            b1lo[:, at(z, 128)] = lo
            for j in range(3):
                hi, lo = split(rb1[:, j].reshape(512, NORB))
                b1hi[:, at((z + j + 1) % 4, 128)] = hi
                b1lo[:, at((z + j + 1) % 4, 128)] = lo

        k1 = i - LAG_1

        @pl.when(valid(k1))
        def _():
            for j in range(1, 4):
                b = (x + j) % 4
                ref = a1.at[b, at(k1, LINE)]
                remote(ref, ref, a1_send.at[0], a1_recv.at[b, k1], at_right).wait_recv()
            rows = at(k1, LINE)
            total = product(jnp.concatenate([a1[b, rows, :] for b in range(4)], axis=1), b1hi, b1lo)
            for t in range(4):
                q[t, rows, :] = total[:, t * 128:(t + 1) * 128]

        k_r, k_l = k1 - z * HOP, k1 - (3 - z) * HOP
        for t in range(4):
            for way, k, first, mine, into in ((0, k_r, z > 0, t > z, into_r), (1, k_l, z < 3, t < z, into_l)):
                @pl.when(valid(k) & first & mine)
                def _(t=t, way=way, k=k, into=into):
                    onward(t, k, way).wait_recv()
                    rows = at(k, LINE)
                    q[t, rows, :] = q[t, rows, :] + into[t, rows, :]

        k2 = i - LAG_2

        @pl.when(valid(k2))
        def _():
            @pl.when(z == 3)
            def _():
                got_2(0, k2)

            @pl.when(z == 0)
            def _():
                got_2(3, k2)

            rows = at(k2, LINE)
            total = product(jnp.concatenate([a2[b, rows, :] for b in range(4)], axis=1), b2hi, b2lo)
            for t in range(4):
                p2[t, rows, :] = total[:, t * 128:(t + 1) * 128]

        for t in range(4):
            for way, k, mine in ((0, k_r, (t > z) & (z < 3)), (1, k_l, (t < z) & (z > 0))):
                @pl.when(valid(k) & mine)
                def _(t=t, way=way, k=k):
                    onward(t, k, way).start()

        f1, f2 = i - DONE_1, i - DONE_2

        @pl.when((f1 >= 1) & (f1 < 9))
        def _():
            ref = at(f1 - 1, LINE)
            remote(rotated.at[ref], halo.at[1, ref], h_send.at[0], h_recv.at[1], at_prev).start()

        @pl.when((f2 >= 1) & (f2 < 9))
        def _():
            remote(rotated.at[at(f2 - 1 + 16, LINE)], halo.at[0, at(f2 - 1, LINE)],
                   h_send.at[1], h_recv.at[0], at_next).start()

        @pl.when(f1 == 8)
        def _():
            plane_sums(0)

        @pl.when(f2 == 8)
        def _():
            plane_sums(2)

        @pl.when(valid(f2))
        def _():
            rows = at(f2, LINE)
            for j in range(3):
                rs_2(j, f2).wait_recv()
            finish((p2[x, rows, :] + rs2[0, rows, :]) + (rs2[1, rows, :] + rs2[2, rows, :]), line_2(f2))

        @pl.when(valid(f1))
        def _():
            rows = at(f1, LINE)

            @pl.when(z > 0)
            def _():
                onward(z, f1, 0).wait_recv()
                q[z, rows, :] = q[z, rows, :] + into_r[z, rows, :]

            @pl.when(z < 3)
            def _():
                onward(z, f1, 1).wait_recv()
                q[z, rows, :] = q[z, rows, :] + into_l[z, rows, :]

            finish(q[z, rows, :], f1)

        @pl.when(valid(k2))
        def _():
            for j in range(3):
                rs_2(j, k2).start()

        return 0

    lax.fori_loop(0, N + DONE_1, step, 0)

    half = pl.ds(0, HALF)
    for j in range(3):
        remote(a1.at[x], a1.at[x], a1_send.at[j], a1_recv.at[0, 0], x_peers[j]).wait_send()
    for b in range(4):
        for way, out, on in ((0, (z < 3) & (b <= z), (z < 3) & (b > z)), (1, (z > 0) & (b >= z), (z > 0) & (b < z))):
            @pl.when(out)
            def _(b=b, way=way):
                remote(a2.at[b], a2.at[b], a2_send.at[way, b], a2_recv.at[0, 0], at_right).wait_send()

            @pl.when(on)
            def _(b=b, way=way):
                sem = l_send if way else r_send
                remote(q.at[b], q.at[b], sem.at[b], r_recv.at[0, 0], at_right).wait_send()

    plane_sums(1)

    remote(halo.at[0], halo.at[0], h_send.at[0], h_recv.at[0], at_next).wait_recv()
    remote(halo.at[1], halo.at[1], h_send.at[0], h_recv.at[1], at_next).wait_recv()

    for p in range(3):
        for line in range(8):
            rows = pl.ds(line * LINE, LINE)
            here = pl.ds((p * 8 + line) * LINE, LINE)
            r = rotated[here, :]
            total = rotated[pl.ds(((p - 1) * 8 + line) * LINE, LINE), :] if p > 0 else halo[0, rows, :]
            total += rotated[pl.ds(((p + 1) * 8 + line) * LINE, LINE), :] if p < 2 else halo[1, rows, :]
            total += rotated[pl.ds((p * 8 + (line + 1) % 8) * LINE, LINE), :]
            total += rotated[pl.ds((p * 8 + (line + 7) % 8) * LINE, LINE), :]
            total += pltpu.roll(r, 1, 0) + pltpu.roll(r, LINE - 1, 0)
            hpsi[here, :] = 3.0 * r - 0.5 * total

    sums = []
    for p in range(3):
        from_all(dx.at[p], d_send.at[p], d_recv.at[p], orb_peers).wait_recv()
        total = dpart[p * 8:p * 8 + 8]
        for j in range(15):
            total += dx[p, j]
        sums.append(total)
    density = jnp.concatenate(sums, axis=0) * (1.0 / M)
    dens[...] = density
    pot = vloc[...] - (3.0 / jnp.pi) ** (1.0 / 3.0) * cbrt(density)
    turned = jnp.concatenate([pot, jnp.zeros((LINE - NLINE, LINE), jnp.float32)], axis=0).T

    acc = jnp.zeros((8, NORB), jnp.float32)
    for n in range(NLINE):
        rows = pl.ds(n * LINE, LINE)
        r = rotated[rows, :]
        h = hpsi[rows, :] + jnp.broadcast_to(turned[:, n:n + 1], (LINE, NORB)) * r
        hpsi[rows, :] = h
        acc += jnp.sum((r * h).reshape(LINE // 8, 8, NORB), axis=0)
    bpart[...] = acc
    for p in range(3):
        from_all(dx.at[p], d_send.at[p], d_recv.at[p], orb_peers).wait_send()
    to_all(bpart, bx, b_send.at[0], b_recv.at[0], dom_peers)
    shared = from_all(bx, b_send.at[0], b_recv.at[0], dom_peers)
    shared.wait_recv()
    total = acc
    for j in range(15):
        total += bx[j]
    band[...] = jnp.sum(total, axis=0, keepdims=True) * (1.0 / NPTS)
    shared.wait_send()

    for j in range(3):
        rot_1(j).wait_send()
        for n in range(2):
            rot_2(j, n).wait_send()
        remote(p2.at[0], p2.at[0], rs_send.at[j], rs_recv.at[0, 0], x_peers[j]).wait_send()
    for j in range(7):
        share_1(j).wait_send()
    share_2.wait_send()
    for side in range(2):
        remote(halo.at[0], halo.at[0], h_send.at[side], h_recv.at[0], at_next).wait_send()


def put_kernel(*refs):
    count = len(refs) // 2
    sem = refs[-1]
    copies = [pltpu.make_async_copy(refs[n], refs[count + n], sem.at[n]) for n in range(count)]
    for copy in copies:
        copy.start()
    for copy in copies:
        copy.wait()


def put(*arrays):
    hbm = pl.BlockSpec(memory_space=pl.ANY)
    return pl.pallas_call(
        put_kernel,
        out_shape=tuple(jax.ShapeDtypeStruct(a.shape, a.dtype) for a in arrays),
        in_specs=[hbm] * len(arrays),
        out_specs=(hbm,) * len(arrays),
        scratch_shapes=[pltpu.SemaphoreType.DMA((len(arrays),))],
        compiler_params=pltpu.CompilerParams(vmem_limit_bytes=16 * 1024 * 1024),
        name="put",
    )(*arrays)


def shards(psi, rot, occ, v_loc):
    f32 = jnp.float32
    vmem, hbm = pl.BlockSpec(memory_space=pltpu.VMEM), pl.BlockSpec(memory_space=pltpu.HBM)
    dma = pltpu.SemaphoreType.DMA
    rotated, density, hpsi, band = pl.pallas_call(
        kernel,
        out_shape=(
            jax.ShapeDtypeStruct((PTS, NORB), f32),
            jax.ShapeDtypeStruct((NLINE, LINE), f32),
            jax.ShapeDtypeStruct((PTS, NORB), f32),
            jax.ShapeDtypeStruct((1, NORB), f32),
        ),
        in_specs=[hbm] * 4,
        out_specs=(vmem, vmem, vmem, vmem),
        scratch_shapes=[
            pltpu.VMEM((1, NORB), f32),
            pltpu.VMEM((NLINE, LINE), f32),
            pltpu.VMEM((4, HALF, NORB), f32),
            pltpu.VMEM((4, HALF, NORB), f32),
            pltpu.VMEM((M, NORB), f32),
            pltpu.VMEM((8, 3, 64, NORB), f32),
            pltpu.VMEM((2, 3, 2, 128, NORB), f32),
            pltpu.VMEM((512, 512), jnp.bfloat16),
            pltpu.VMEM((512, 512), jnp.bfloat16),
            pltpu.VMEM((512, 512), jnp.bfloat16),
            pltpu.VMEM((512, 512), jnp.bfloat16),
            pltpu.VMEM((4, HALF, NORB), f32),
            pltpu.VMEM((4, HALF, NORB), f32),
            pltpu.VMEM((4, HALF, NORB), f32),
            pltpu.VMEM((4, HALF, NORB), f32),
            pltpu.VMEM((3, HALF, NORB), f32),
            pltpu.VMEM((2, 1024, NORB), f32),
            pltpu.VMEM((NLINE, LINE), f32),
            pltpu.VMEM((3, 15, 8, LINE), f32),
            pltpu.VMEM((8, NORB), f32),
            pltpu.VMEM((15, 8, NORB), f32),
            dma((6,)),
            dma((4, N)),
            dma((3,)),
            dma((4, N)),
            dma((2, 4)),
            dma((3,)),
            dma((3,)),
            dma((7,)),
            dma((8,)),
            dma((3, 2)),
            dma((3, 2)),
            dma((2,)),
            dma((4, N)),
            dma((4,)),
            dma((4, N)),
            dma((4,)),
            dma((3, N)),
            dma((3,)),
            dma((2,)),
            dma((2,)),
            dma((3,)),
            dma((3,)),
            dma((1,)),
            dma((1,)),
        ],
        compiler_params=pltpu.CompilerParams(
            collective_id=0, has_side_effects=True, vmem_limit_bytes=40 * 1024 * 1024),
        name="rotate",
    )(*[pltpu.with_memory_space_constraint(v, pltpu.HBM) for v in (
        psi, rot, occ.reshape(1, NORB), v_loc.reshape(NLINE, LINE))])
    return put(rotated, density.reshape(PTS), hpsi, band.reshape(NORB))


def solution(mesh):
    placed = (P("dom", "orb"), P(None, "orb"), P("orb"), P("dom"))
    return jax.shard_map(
        shards,
        mesh=mesh,
        in_specs=placed,
        out_specs=(P("dom", "orb"), P("dom"), P("dom", "orb"), P("orb")),
        check_vma=False,
    )
```

```python
import jax
import jax.numpy as jnp
from jax import lax
from jax.experimental import pallas as pl
from jax.experimental.pallas import tpu as pltpu
from jax.sharding import PartitionSpec as P

M = 2048
PTS = 3072
NORB = 128
NLINE = 24
LINE = 128
NPTS = 49152
N = 12
HALF = N * LINE
AHEAD1 = 3
AHEAD2 = 4
LAG_1 = 2
HOP = 1
DONE_1 = LAG_1 + 3 * HOP
LAG_2 = 3
DONE_2 = 4
LATE_1 = 4
LATE_2 = 5

MESH = pl.DeviceIdType.MESH
HIGHEST = lax.Precision.HIGHEST


def line_2(k):
    return k + 16 - 12 * (k // 8)


def split(v):
    hi = v.astype(jnp.bfloat16)
    return hi, (v - hi.astype(jnp.float32)).astype(jnp.bfloat16)


def cbrt(d):
    safe = jnp.maximum(d, 1e-37)
    y = jnp.exp(jnp.log(safe) * (1.0 / 3.0))
    y = y - (y - safe / (y * y)) * (1.0 / 3.0)
    return jnp.where(d < 1e-37, 0.0, y)


def kernel(psi, rot, occ_hbm, vloc_hbm, rotated, dens, hpsi, band,
           occ, vloc, a1, a2, rotv, rb1, rb2, b1hi, b1lo, b2hi, b2lo, q, into_r, into_l, p2, rs2, halo, dpart, dx, bpart, bx,
           in_sem, a1_recv, a1_send, a2_recv, a2_send, r1_send, r1_recv, s1_send, s1_recv, r2_send, r2_recv, s2_sem,
           r_recv, r_send, l_recv, l_send, rs_recv, rs_send, h_recv, h_send, d_send, d_recv, b_send, b_recv):
    dom = lax.axis_index("dom")
    orb = lax.axis_index("orb")
    y, zh, c = dom // 4, (dom // 2) % 2, dom % 2
    z, x = orb // 4, orb % 4
    at_right, at_left = (dom, ((z + 1) % 4) * 4 + x), (dom, ((z + 3) % 4) * 4 + x)
    at_prev, at_next = ((dom + 15) % 16, orb), ((dom + 1) % 16, orb)
    at_twin = (dom + 1 - 2 * c, orb)
    e = y * 2 + c

    def at_yc(f):
        return ((f // 2) * 4 + zh * 2 + f % 2, orb)

    x_peers = [(dom, z * 4 + (x + j) % 4) for j in (1, 2, 3)]
    z_peers = [(dom, ((z + j) % 4) * 4 + x) for j in (1, 2, 3)]
    orb_peers = [(dom, (orb + j) % 16) for j in range(1, 16)]
    dom_peers = [((dom + j) % 16, orb) for j in range(1, 16)]
    yc_peers = [at_yc((e + j) % 8) for j in range(1, 8)]

    loads = [pltpu.make_async_copy(src, dst, in_sem.at[n]) for n, (src, dst) in enumerate([
        (psi.at[pl.ds(0, HALF)], a1.at[x]),
        (psi.at[pl.ds(2048, 1024)], a2.at[z, pl.ds(0, 1024)]),
        (psi.at[pl.ds(HALF, 512)], a2.at[z, pl.ds(1024, 512)]),
        (rot, rotv), (occ_hbm, occ), (vloc_hbm, vloc)])]
    for load in loads:
        load.start()

    barrier = pltpu.get_barrier_semaphore()
    everyone = orb_peers + dom_peers
    for peer in everyone:
        pl.semaphore_signal(barrier, inc=1, device_id=peer, device_id_type=MESH)
    pl.semaphore_wait(barrier, len(everyone))
    for load in loads:
        load.wait()

    def remote(src, dst, send, recv, peer):
        return pltpu.make_async_remote_copy(
            src_ref=src, dst_ref=dst, send_sem=send, recv_sem=recv, device_id=peer, device_id_type=MESH)

    def at(n, size):
        return pl.ds(pl.multiple_of(n * size, size), size)

    def send_1(k):
        ref = a1.at[x, at(k, LINE)]
        for j in range(3):
            remote(ref, ref, a1_send.at[j], a1_recv.at[x, k], x_peers[j]).start()

    def block_2(b, k, way):
        ref = a2.at[b, at(k, LINE)]
        return remote(ref, ref, a2_send.at[way, b], a2_recv.at[b, k], at_left if way else at_right)

    def got_2(b, k):
        block_2(b, k, 0).wait_recv()

    def send_2(k):
        @pl.when(z < 3)
        def _():
            block_2(z, k, 0).start()

        @pl.when(z > 0)
        def _():
            block_2(z, k, 1).start()

    def rot_1(j):
        return remote(rotv.at[at(((z + j + 1) % 4) * 8 + e, 64)], rb1.at[e, 2 - j],
                      r1_send.at[j], r1_recv.at[2 - j], z_peers[j])

    def share_1(j):
        return remote(rb1.at[e], rb1.at[e], s1_send.at[j], s1_recv.at[e], yc_peers[j])

    def rot_2(j, n):
        return remote(rotv.at[at((2 * c + n) * 4 + (x + j + 1) % 4, 128)], rb2.at[c, 2 - j, n],
                      r2_send.at[j, n], r2_recv.at[2 - j, n], x_peers[j])

    share_2 = remote(rb2.at[c], rb2.at[c], s2_sem.at[0], s2_sem.at[1], at_twin)

    send_2(0)
    for j in range(3):
        rot_1(j).start()
    for j in range(3):
        for n in range(2):
            rot_2(j, n).start()
    for k in range(1, AHEAD2):
        send_2(k)
    for k in range(AHEAD1):
        send_1(k)

    def onward(t, k, way):
        rows = at(k, LINE)
        if way == 0:
            return remote(q.at[t, rows], into_r.at[t, rows], r_send.at[t], r_recv.at[t, k], at_right)
        return remote(q.at[t, rows], into_l.at[t, rows], l_send.at[t], l_recv.at[t, k], at_left)

    def rs_2(j, k):
        rows = at(k, LINE)
        return remote(p2.at[(x + j + 1) % 4, rows], rs2.at[2 - j, rows], rs_send.at[j], rs_recv.at[2 - j, k], x_peers[j])

    def to_all(src, dst, send, recv, peers):
        for j, peer in enumerate(peers):
            remote(src, dst.at[14 - j], send, recv, peer).start()

    def from_all(dst, send, recv, peers):
        return remote(dst, dst, send, recv, peers[0])

    def plane_sums(p):
        to_all(dpart.at[pl.ds(p * 8, 8)], dx.at[p], d_send.at[p], d_recv.at[p], orb_peers)

    def product(a, hi_ref, lo_ref):
        hi, lo = split(a)
        total = jnp.dot(hi, lo_ref[...], preferred_element_type=jnp.float32)
        total += jnp.dot(lo, hi_ref[...], preferred_element_type=jnp.float32)
        return total + jnp.dot(hi, hi_ref[...], preferred_element_type=jnp.float32)

    def finish(r, line):
        rotated[at(line, LINE), :] = r
        d = lax.dot_general(jnp.broadcast_to(occ[...], (8, NORB)), r * r, (((1,), (1,)), ((), ())),
                            precision=HIGHEST, preferred_element_type=jnp.float32)
        dpart[pl.ds(line, 1), :] = d[0:1]

    def valid(k):
        return (k >= 0) & (k < N)

    def step(i, _):
        @pl.when(i + AHEAD2 < N)
        def _():
            send_2(i + AHEAD2)

        @pl.when(i + AHEAD1 < N)
        def _():
            send_1(i + AHEAD1)

        for hop in (1, 2):
            k = i - hop + 1

            @pl.when(valid(k) & (z >= hop))
            def _(hop=hop, k=k):
                got_2(z - hop, k)

                @pl.when(z < 3)
                def _():
                    block_2(z - hop, k, 0).start()

            @pl.when(valid(k) & (z <= 3 - hop))
            def _(hop=hop, k=k):
                got_2(z + hop, k)

                @pl.when(z > 0)
                def _():
                    block_2(z + hop, k, 1).start()

        @pl.when(i == 0)
        def _():
            for j in range(3):
                rot_1(j).wait_recv()
            for j in range(7):
                share_1(j).start()

        @pl.when(i == 1)
        def _():
            for j in range(3):
                for n in range(2):
                    rot_2(j, n).wait_recv()
            share_2.start()

        @pl.when(i == LAG_2)
        def _():
            share_2.wait_recv()
            for n in range(4):
                hi, lo = split(rotv[at(n * 4 + x, 128), :])
                b2hi[pl.ds(n * 128, 128), at(x, 128)] = hi
                b2lo[pl.ds(n * 128, 128), at(x, 128)] = lo
            for j in range(3):
                hi, lo = split(rb2[:, j].reshape(512, NORB))
                b2hi[:, at((x + j + 1) % 4, 128)] = hi
                b2lo[:, at((x + j + 1) % 4, 128)] = lo

        @pl.when(i == LAG_1)
        def _():
            for j in range(1, 8):
                f = (e + j) % 8
                remote(rb1.at[f], rb1.at[f], s1_send.at[0], s1_recv.at[f], at_twin).wait_recv()
            hi, lo = split(rotv[at(z, 512), :])
            b1hi[:, at(z, 128)] = hi
            b1lo[:, at(z, 128)] = lo
            for j in range(3):
                hi, lo = split(rb1[:, j].reshape(512, NORB))
                b1hi[:, at((z + j + 1) % 4, 128)] = hi
                b1lo[:, at((z + j + 1) % 4, 128)] = lo

        k1 = i - LAG_1

        @pl.when(valid(k1))
        def _():
            for j in range(1, 4):
                b = (x + j) % 4
                ref = a1.at[b, at(k1, LINE)]
                remote(ref, ref, a1_send.at[0], a1_recv.at[b, k1], at_right).wait_recv()
            rows = at(k1, LINE)
            total = product(jnp.concatenate([a1[b, rows, :] for b in range(4)], axis=1), b1hi, b1lo)
            for t in range(4):
                q[t, rows, :] = total[:, t * 128:(t + 1) * 128]

        k_r, k_l = k1 - z * HOP, k1 - (3 - z) * HOP
        for t in range(4):
            for way, k, first, mine, into in ((0, k_r, z > 0, t > z, into_r), (1, k_l, z < 3, t < z, into_l)):
                @pl.when(valid(k) & first & mine)
                def _(t=t, way=way, k=k, into=into):
                    onward(t, k, way).wait_recv()
                    rows = at(k, LINE)
                    q[t, rows, :] = q[t, rows, :] + into[t, rows, :]

        k2 = i - LAG_2

        @pl.when(valid(k2))
        def _():
            @pl.when(z == 3)
            def _():
                got_2(0, k2)

            @pl.when(z == 0)
            def _():
                got_2(3, k2)

            rows = at(k2, LINE)
            total = product(jnp.concatenate([a2[b, rows, :] for b in range(4)], axis=1), b2hi, b2lo)
            for t in range(4):
                p2[t, rows, :] = total[:, t * 128:(t + 1) * 128]

        for t in range(4):
            for way, k, mine in ((0, k_r, (t > z) & (z < 3)), (1, k_l, (t < z) & (z > 0))):
                @pl.when(valid(k) & mine)
                def _(t=t, way=way, k=k):
                    onward(t, k, way).start()

        f1, f2 = i - DONE_1, i - DONE_2

        g1, g2 = f1 - LATE_1, f2 - LATE_2

        @pl.when((g1 >= 0) & (g1 < 8))
        def _():
            ref = at(g1, LINE)
            remote(rotated.at[ref], halo.at[1, ref], h_send.at[0], h_recv.at[1], at_prev).start()

        @pl.when((g2 >= 0) & (g2 < 8))
        def _():
            remote(rotated.at[at(g2 + 16, LINE)], halo.at[0, at(g2, LINE)],
                   h_send.at[1], h_recv.at[0], at_next).start()

        @pl.when(f1 == 8)
        def _():
            plane_sums(0)

        @pl.when(f2 == 8)
        def _():
            plane_sums(2)

        @pl.when(valid(f2))
        def _():
            rows = at(f2, LINE)
            for j in range(3):
                rs_2(j, f2).wait_recv()
            finish((p2[x, rows, :] + rs2[0, rows, :]) + (rs2[1, rows, :] + rs2[2, rows, :]), line_2(f2))

        @pl.when(valid(f1))
        def _():
            rows = at(f1, LINE)

            @pl.when(z > 0)
            def _():
                onward(z, f1, 0).wait_recv()
                q[z, rows, :] = q[z, rows, :] + into_r[z, rows, :]

            @pl.when(z < 3)
            def _():
                onward(z, f1, 1).wait_recv()
                q[z, rows, :] = q[z, rows, :] + into_l[z, rows, :]

            finish(q[z, rows, :], f1)

        @pl.when(valid(k2))
        def _():
            for j in range(3):
                rs_2(j, k2).start()

        return 0

    lax.fori_loop(0, max(N + DONE_1, 8 + DONE_1 + LATE_1, 8 + DONE_2 + LATE_2), step, 0)

    half = pl.ds(0, HALF)
    for j in range(3):
        remote(a1.at[x], a1.at[x], a1_send.at[j], a1_recv.at[0, 0], x_peers[j]).wait_send()
    for b in range(4):
        for way, out, on in ((0, (z < 3) & (b <= z), (z < 3) & (b > z)), (1, (z > 0) & (b >= z), (z > 0) & (b < z))):
            @pl.when(out)
            def _(b=b, way=way):
                remote(a2.at[b], a2.at[b], a2_send.at[way, b], a2_recv.at[0, 0], at_right).wait_send()

            @pl.when(on)
            def _(b=b, way=way):
                sem = l_send if way else r_send
                remote(q.at[b], q.at[b], sem.at[b], r_recv.at[0, 0], at_right).wait_send()

    plane_sums(1)

    remote(halo.at[0], halo.at[0], h_send.at[0], h_recv.at[0], at_next).wait_recv()
    remote(halo.at[1], halo.at[1], h_send.at[0], h_recv.at[1], at_next).wait_recv()

    for p in range(3):
        for line in range(8):
            rows = pl.ds(line * LINE, LINE)
            here = pl.ds((p * 8 + line) * LINE, LINE)
            r = rotated[here, :]
            total = rotated[pl.ds(((p - 1) * 8 + line) * LINE, LINE), :] if p > 0 else halo[0, rows, :]
            total += rotated[pl.ds(((p + 1) * 8 + line) * LINE, LINE), :] if p < 2 else halo[1, rows, :]
            total += rotated[pl.ds((p * 8 + (line + 1) % 8) * LINE, LINE), :]
            total += rotated[pl.ds((p * 8 + (line + 7) % 8) * LINE, LINE), :]
            total += pltpu.roll(r, 1, 0) + pltpu.roll(r, LINE - 1, 0)
            hpsi[here, :] = 3.0 * r - 0.5 * total

    acc = jnp.zeros((8, NORB), jnp.float32)
    for p in (0, 2, 1):
        from_all(dx.at[p], d_send.at[p], d_recv.at[p], orb_peers).wait_recv()
        eight = pl.ds(p * 8, 8)
        density = dpart[eight, :]
        for j in range(15):
            density += dx[p, j]
        density = density * (1.0 / M)
        dens[eight, :] = density
        pot = vloc[eight, :] - (3.0 / jnp.pi) ** (1.0 / 3.0) * cbrt(density)
        turned = jnp.concatenate([pot, jnp.zeros((LINE - 8, LINE), jnp.float32)], axis=0).T
        for n in range(8):
            rows = pl.ds((p * 8 + n) * LINE, LINE)
            r = rotated[rows, :]
            h = hpsi[rows, :] + jnp.broadcast_to(turned[:, n:n + 1], (LINE, NORB)) * r
            hpsi[rows, :] = h
            acc += jnp.sum((r * h).reshape(LINE // 8, 8, NORB), axis=0)
    bpart[...] = acc
    for p in range(3):
        from_all(dx.at[p], d_send.at[p], d_recv.at[p], orb_peers).wait_send()
    to_all(bpart, bx, b_send.at[0], b_recv.at[0], dom_peers)
    shared = from_all(bx, b_send.at[0], b_recv.at[0], dom_peers)
    shared.wait_recv()
    total = acc
    for j in range(15):
        total += bx[j]
    band[...] = jnp.sum(total, axis=0, keepdims=True) * (1.0 / NPTS)
    shared.wait_send()

    for j in range(3):
        rot_1(j).wait_send()
        for n in range(2):
            rot_2(j, n).wait_send()
        remote(p2.at[0], p2.at[0], rs_send.at[j], rs_recv.at[0, 0], x_peers[j]).wait_send()
    for j in range(7):
        share_1(j).wait_send()
    share_2.wait_send()
    for side in range(2):
        remote(halo.at[0], halo.at[0], h_send.at[side], h_recv.at[0], at_next).wait_send()


def put_kernel(*refs):
    count = len(refs) // 2
    sem = refs[-1]
    copies = [pltpu.make_async_copy(refs[n], refs[count + n], sem.at[n]) for n in range(count)]
    for copy in copies:
        copy.start()
    for copy in copies:
        copy.wait()


def put(*arrays):
    hbm = pl.BlockSpec(memory_space=pl.ANY)
    return pl.pallas_call(
        put_kernel,
        out_shape=tuple(jax.ShapeDtypeStruct(a.shape, a.dtype) for a in arrays),
        in_specs=[hbm] * len(arrays),
        out_specs=(hbm,) * len(arrays),
        scratch_shapes=[pltpu.SemaphoreType.DMA((len(arrays),))],
        compiler_params=pltpu.CompilerParams(vmem_limit_bytes=16 * 1024 * 1024),
        name="put",
    )(*arrays)


def shards(psi, rot, occ, v_loc):
    f32 = jnp.float32
    vmem, hbm = pl.BlockSpec(memory_space=pltpu.VMEM), pl.BlockSpec(memory_space=pltpu.HBM)
    dma = pltpu.SemaphoreType.DMA
    rotated, density, hpsi, band = pl.pallas_call(
        kernel,
        out_shape=(
            jax.ShapeDtypeStruct((PTS, NORB), f32),
            jax.ShapeDtypeStruct((NLINE, LINE), f32),
            jax.ShapeDtypeStruct((PTS, NORB), f32),
            jax.ShapeDtypeStruct((1, NORB), f32),
        ),
        in_specs=[hbm] * 4,
        out_specs=(vmem, vmem, vmem, vmem),
        scratch_shapes=[
            pltpu.VMEM((1, NORB), f32),
            pltpu.VMEM((NLINE, LINE), f32),
            pltpu.VMEM((4, HALF, NORB), f32),
            pltpu.VMEM((4, HALF, NORB), f32),
            pltpu.VMEM((M, NORB), f32),
            pltpu.VMEM((8, 3, 64, NORB), f32),
            pltpu.VMEM((2, 3, 2, 128, NORB), f32),
            pltpu.VMEM((512, 512), jnp.bfloat16),
            pltpu.VMEM((512, 512), jnp.bfloat16),
            pltpu.VMEM((512, 512), jnp.bfloat16),
            pltpu.VMEM((512, 512), jnp.bfloat16),
            pltpu.VMEM((4, HALF, NORB), f32),
            pltpu.VMEM((4, HALF, NORB), f32),
            pltpu.VMEM((4, HALF, NORB), f32),
            pltpu.VMEM((4, HALF, NORB), f32),
            pltpu.VMEM((3, HALF, NORB), f32),
            pltpu.VMEM((2, 1024, NORB), f32),
            pltpu.VMEM((NLINE, LINE), f32),
            pltpu.VMEM((3, 15, 8, LINE), f32),
            pltpu.VMEM((8, NORB), f32),
            pltpu.VMEM((15, 8, NORB), f32),
            dma((6,)),
            dma((4, N)),
            dma((3,)),
            dma((4, N)),
            dma((2, 4)),
            dma((3,)),
            dma((3,)),
            dma((7,)),
            dma((8,)),
            dma((3, 2)),
            dma((3, 2)),
            dma((2,)),
            dma((4, N)),
            dma((4,)),
            dma((4, N)),
            dma((4,)),
            dma((3, N)),
            dma((3,)),
            dma((2,)),
            dma((2,)),
            dma((3,)),
            dma((3,)),
            dma((1,)),
            dma((1,)),
        ],
        compiler_params=pltpu.CompilerParams(
            collective_id=0, has_side_effects=True, vmem_limit_bytes=40 * 1024 * 1024),
        name="rotate",
    )(*[pltpu.with_memory_space_constraint(v, pltpu.HBM) for v in (
        psi, rot, occ.reshape(1, NORB), v_loc.reshape(NLINE, LINE))])
    return put(rotated, density.reshape(PTS), hpsi, band.reshape(NORB))


def solution(mesh):
    placed = (P("dom", "orb"), P(None, "orb"), P("orb"), P("dom"))
    return jax.shard_map(
        shards,
        mesh=mesh,
        in_specs=placed,
        out_specs=(P("dom", "orb"), P("dom"), P("dom", "orb"), P("orb")),
        check_vma=False,
    )
```

```python
import jax
import jax.numpy as jnp
from jax import lax
from jax.experimental import pallas as pl
from jax.experimental.pallas import tpu as pltpu
from jax.sharding import PartitionSpec as P

M = 2048
TINY = 1.1754944e-38
PTS = 3072
NORB = 128
NLINE = 24
LINE = 128
NPTS = 49152
N = 12
HALF = N * LINE
AHEAD1 = 3
AHEAD2 = 4
LAG_1 = 2
HOP = 1
DONE_1 = LAG_1 + 3 * HOP
LAG_2 = 3
DONE_2 = 4
LATE_1 = 4
LATE_2 = 5

MESH = pl.DeviceIdType.MESH
HIGHEST = lax.Precision.HIGHEST


def line_2(k):
    return k + 16 - 12 * (k // 8)


def split(v):
    hi = v.astype(jnp.bfloat16)
    return hi, (v - hi.astype(jnp.float32)).astype(jnp.bfloat16)


def cbrt(d):
    safe = jnp.maximum(d, TINY)
    y = jnp.exp(jnp.log(safe) * (1.0 / 3.0))
    y = y - (y - safe / (y * y)) * (1.0 / 3.0)
    return jnp.where(d < TINY, 0.0, y)


def kernel(psi, rot, occ_hbm, vloc_hbm, rotated, dens, hpsi, band,
           occ, vloc, a1, a2, rotv, rb1, rb2, b1hi, b1lo, b2hi, b2lo, q, into_r, into_l, p2, rs2, halo, dpart, dx, bpart, bx,
           in_sem, a1_recv, a1_send, a2_recv, a2_send, r1_send, r1_recv, s1_send, s1_recv, r2_send, r2_recv, s2_sem,
           r_recv, r_send, l_recv, l_send, rs_recv, rs_send, h_recv, h_send, d_send, d_recv, b_send, b_recv):
    dom = lax.axis_index("dom")
    orb = lax.axis_index("orb")
    y, zh, c = dom // 4, (dom // 2) % 2, dom % 2
    z, x = orb // 4, orb % 4
    at_right, at_left = (dom, ((z + 1) % 4) * 4 + x), (dom, ((z + 3) % 4) * 4 + x)
    at_prev, at_next = ((dom + 15) % 16, orb), ((dom + 1) % 16, orb)
    at_twin = (dom + 1 - 2 * c, orb)
    e = y * 2 + c

    def at_yc(f):
        return ((f // 2) * 4 + zh * 2 + f % 2, orb)

    x_peers = [(dom, z * 4 + (x + j) % 4) for j in (1, 2, 3)]
    z_peers = [(dom, ((z + j) % 4) * 4 + x) for j in (1, 2, 3)]
    orb_peers = [(dom, (orb + j) % 16) for j in range(1, 16)]
    dom_peers = [((dom + j) % 16, orb) for j in range(1, 16)]
    yc_peers = [at_yc((e + j) % 8) for j in range(1, 8)]

    loads = [pltpu.make_async_copy(src, dst, in_sem.at[n]) for n, (src, dst) in enumerate([
        (psi.at[pl.ds(0, HALF)], a1.at[x]),
        (psi.at[pl.ds(2048, 1024)], a2.at[z, pl.ds(0, 1024)]),
        (psi.at[pl.ds(HALF, 512)], a2.at[z, pl.ds(1024, 512)]),
        (rot, rotv), (occ_hbm, occ), (vloc_hbm, vloc)])]
    for load in loads:
        load.start()

    barrier = pltpu.get_barrier_semaphore()
    everyone = orb_peers + dom_peers
    for peer in everyone:
        pl.semaphore_signal(barrier, inc=1, device_id=peer, device_id_type=MESH)
    pl.semaphore_wait(barrier, len(everyone))
    for load in loads:
        load.wait()

    def remote(src, dst, send, recv, peer):
        return pltpu.make_async_remote_copy(
            src_ref=src, dst_ref=dst, send_sem=send, recv_sem=recv, device_id=peer, device_id_type=MESH)

    def at(n, size):
        return pl.ds(pl.multiple_of(n * size, size), size)

    def send_1(k):
        ref = a1.at[x, at(k, LINE)]
        for j in range(3):
            remote(ref, ref, a1_send.at[j], a1_recv.at[x, k], x_peers[j]).start()

    def block_2(b, k, way):
        ref = a2.at[b, at(k, LINE)]
        return remote(ref, ref, a2_send.at[way, b], a2_recv.at[b, k], at_left if way else at_right)

    def got_2(b, k):
        block_2(b, k, 0).wait_recv()

    def send_2(k):
        @pl.when(z < 3)
        def _():
            block_2(z, k, 0).start()

        @pl.when(z > 0)
        def _():
            block_2(z, k, 1).start()

    def rot_1(j):
        return remote(rotv.at[at(((z + j + 1) % 4) * 8 + e, 64)], rb1.at[e, 2 - j],
                      r1_send.at[j], r1_recv.at[2 - j], z_peers[j])

    def share_1(j):
        return remote(rb1.at[e], rb1.at[e], s1_send.at[j], s1_recv.at[e], yc_peers[j])

    def rot_2(j, n):
        return remote(rotv.at[at((2 * c + n) * 4 + (x + j + 1) % 4, 128)], rb2.at[c, 2 - j, n],
                      r2_send.at[j, n], r2_recv.at[2 - j, n], x_peers[j])

    share_2 = remote(rb2.at[c], rb2.at[c], s2_sem.at[0], s2_sem.at[1], at_twin)

    send_2(0)
    for j in range(3):
        rot_1(j).start()
    for j in range(3):
        for n in range(2):
            rot_2(j, n).start()
    for k in range(1, AHEAD2):
        send_2(k)
    for k in range(AHEAD1):
        send_1(k)

    def onward(t, k, way):
        rows = at(k, LINE)
        if way == 0:
            return remote(q.at[t, rows], into_r.at[t, rows], r_send.at[t], r_recv.at[t, k], at_right)
        return remote(q.at[t, rows], into_l.at[t, rows], l_send.at[t], l_recv.at[t, k], at_left)

    def rs_2(j, k):
        rows = at(k, LINE)
        return remote(p2.at[(x + j + 1) % 4, rows], rs2.at[2 - j, rows], rs_send.at[j], rs_recv.at[2 - j, k], x_peers[j])

    def to_all(src, dst, send, recv, peers):
        for j, peer in enumerate(peers):
            remote(src, dst.at[14 - j], send, recv, peer).start()

    def from_all(dst, send, recv, peers):
        return remote(dst, dst, send, recv, peers[0])

    def plane_sums(p):
        to_all(dpart.at[pl.ds(p * 8, 8)], dx.at[p], d_send.at[p], d_recv.at[p], orb_peers)

    def product(a, hi_ref, lo_ref):
        hi, lo = split(a)
        total = jnp.dot(hi, lo_ref[...], preferred_element_type=jnp.float32)
        total += jnp.dot(lo, hi_ref[...], preferred_element_type=jnp.float32)
        return total + jnp.dot(hi, hi_ref[...], preferred_element_type=jnp.float32)

    def finish(r, line):
        rotated[at(line, LINE), :] = r
        d = lax.dot_general(jnp.broadcast_to(occ[...], (8, NORB)), r * r, (((1,), (1,)), ((), ())),
                            precision=HIGHEST, preferred_element_type=jnp.float32)
        dpart[pl.ds(line, 1), :] = d[0:1]

    def valid(k):
        return (k >= 0) & (k < N)

    def step(i, _):
        for hop in (1, 2):
            k = i - hop + 1

            @pl.when(valid(k) & (z >= hop))
            def _(hop=hop, k=k):
                got_2(z - hop, k)

                @pl.when(z < 3)
                def _():
                    block_2(z - hop, k, 0).start()

            @pl.when(valid(k) & (z <= 3 - hop))
            def _(hop=hop, k=k):
                got_2(z + hop, k)

                @pl.when(z > 0)
                def _():
                    block_2(z + hop, k, 1).start()

        @pl.when(i == 0)
        def _():
            for j in range(3):
                rot_1(j).wait_recv()
            for j in range(7):
                share_1(j).start()

        @pl.when(i == 1)
        def _():
            for j in range(3):
                for n in range(2):
                    rot_2(j, n).wait_recv()
            share_2.start()

        @pl.when(i == LAG_2)
        def _():
            share_2.wait_recv()
            for n in range(4):
                hi, lo = split(rotv[at(n * 4 + x, 128), :])
                b2hi[pl.ds(n * 128, 128), at(x, 128)] = hi
                b2lo[pl.ds(n * 128, 128), at(x, 128)] = lo
            for j in range(3):
                hi, lo = split(rb2[:, j].reshape(512, NORB))
                b2hi[:, at((x + j + 1) % 4, 128)] = hi
                b2lo[:, at((x + j + 1) % 4, 128)] = lo

        @pl.when(i == LAG_1)
        def _():
            for j in range(1, 8):
                f = (e + j) % 8
                remote(rb1.at[f], rb1.at[f], s1_send.at[0], s1_recv.at[f], at_twin).wait_recv()
            hi, lo = split(rotv[at(z, 512), :])
            b1hi[:, at(z, 128)] = hi
            b1lo[:, at(z, 128)] = lo
            for j in range(3):
                hi, lo = split(rb1[:, j].reshape(512, NORB))
                b1hi[:, at((z + j + 1) % 4, 128)] = hi
                b1lo[:, at((z + j + 1) % 4, 128)] = lo

        k1 = i - LAG_1

        @pl.when(valid(k1))
        def _():
            for j in range(1, 4):
                b = (x + j) % 4
                ref = a1.at[b, at(k1, LINE)]
                remote(ref, ref, a1_send.at[0], a1_recv.at[b, k1], at_right).wait_recv()
            rows = at(k1, LINE)
            total = product(jnp.concatenate([a1[b, rows, :] for b in range(4)], axis=1), b1hi, b1lo)
            for t in range(4):
                q[t, rows, :] = total[:, t * 128:(t + 1) * 128]

        k_r, k_l = k1 - z * HOP, k1 - (3 - z) * HOP
        for t in range(4):
            for way, k, first, mine, into in ((0, k_r, z > 0, t > z, into_r), (1, k_l, z < 3, t < z, into_l)):
                @pl.when(valid(k) & first & mine)
                def _(t=t, way=way, k=k, into=into):
                    onward(t, k, way).wait_recv()
                    rows = at(k, LINE)
                    q[t, rows, :] = q[t, rows, :] + into[t, rows, :]

        k2 = i - LAG_2

        @pl.when(valid(k2))
        def _():
            @pl.when(z == 3)
            def _():
                got_2(0, k2)

            @pl.when(z == 0)
            def _():
                got_2(3, k2)

            rows = at(k2, LINE)
            total = product(jnp.concatenate([a2[b, rows, :] for b in range(4)], axis=1), b2hi, b2lo)
            for t in range(4):
                p2[t, rows, :] = total[:, t * 128:(t + 1) * 128]

        for t in range(4):
            for way, k, mine in ((0, k_r, (t > z) & (z < 3)), (1, k_l, (t < z) & (z > 0))):
                @pl.when(valid(k) & mine)
                def _(t=t, way=way, k=k):
                    onward(t, k, way).start()

        @pl.when(i + AHEAD2 < N)
        def _():
            send_2(i + AHEAD2)

        @pl.when(i + AHEAD1 < N)
        def _():
            send_1(i + AHEAD1)

        f1, f2 = i - DONE_1, i - DONE_2

        g1, g2 = f1 - LATE_1, f2 - LATE_2

        @pl.when((g1 >= 0) & (g1 < 8))
        def _():
            ref = at(g1, LINE)
            remote(rotated.at[ref], halo.at[1, ref], h_send.at[0], h_recv.at[1], at_prev).start()

        @pl.when((g2 >= 0) & (g2 < 8))
        def _():
            remote(rotated.at[at(g2 + 16, LINE)], halo.at[0, at(g2, LINE)],
                   h_send.at[1], h_recv.at[0], at_next).start()

        @pl.when(f1 == 8)
        def _():
            plane_sums(0)

        @pl.when(f2 == 8)
        def _():
            plane_sums(2)

        @pl.when(valid(f2))
        def _():
            rows = at(f2, LINE)
            for j in range(3):
                rs_2(j, f2).wait_recv()
            finish((p2[x, rows, :] + rs2[0, rows, :]) + (rs2[1, rows, :] + rs2[2, rows, :]), line_2(f2))

        @pl.when(valid(f1))
        def _():
            rows = at(f1, LINE)

            @pl.when(z > 0)
            def _():
                onward(z, f1, 0).wait_recv()
                q[z, rows, :] = q[z, rows, :] + into_r[z, rows, :]

            @pl.when(z < 3)
            def _():
                onward(z, f1, 1).wait_recv()
                q[z, rows, :] = q[z, rows, :] + into_l[z, rows, :]

            finish(q[z, rows, :], f1)

        @pl.when(valid(k2))
        def _():
            for j in range(3):
                rs_2(j, k2).start()

        return 0

    lax.fori_loop(0, max(N + DONE_1, 8 + DONE_1 + LATE_1, 8 + DONE_2 + LATE_2), step, 0)

    half = pl.ds(0, HALF)
    for j in range(3):
        remote(a1.at[x], a1.at[x], a1_send.at[j], a1_recv.at[0, 0], x_peers[j]).wait_send()
    for b in range(4):
        for way, out, on in ((0, (z < 3) & (b <= z), (z < 3) & (b > z)), (1, (z > 0) & (b >= z), (z > 0) & (b < z))):
            @pl.when(out)
            def _(b=b, way=way):
                remote(a2.at[b], a2.at[b], a2_send.at[way, b], a2_recv.at[0, 0], at_right).wait_send()

            @pl.when(on)
            def _(b=b, way=way):
                sem = l_send if way else r_send
                remote(q.at[b], q.at[b], sem.at[b], r_recv.at[0, 0], at_right).wait_send()

    plane_sums(1)

    remote(halo.at[0], halo.at[0], h_send.at[0], h_recv.at[0], at_next).wait_recv()
    remote(halo.at[1], halo.at[1], h_send.at[0], h_recv.at[1], at_next).wait_recv()

    for p in range(3):
        for line in range(8):
            rows = pl.ds(line * LINE, LINE)
            here = pl.ds((p * 8 + line) * LINE, LINE)
            r = rotated[here, :]
            total = rotated[pl.ds(((p - 1) * 8 + line) * LINE, LINE), :] if p > 0 else halo[0, rows, :]
            total += rotated[pl.ds(((p + 1) * 8 + line) * LINE, LINE), :] if p < 2 else halo[1, rows, :]
            total += rotated[pl.ds((p * 8 + (line + 1) % 8) * LINE, LINE), :]
            total += rotated[pl.ds((p * 8 + (line + 7) % 8) * LINE, LINE), :]
            total += pltpu.roll(r, 1, 0) + pltpu.roll(r, LINE - 1, 0)
            hpsi[here, :] = 3.0 * r - 0.5 * total

    acc = jnp.zeros((8, NORB), jnp.float32)
    for p in (0, 2, 1):
        from_all(dx.at[p], d_send.at[p], d_recv.at[p], orb_peers).wait_recv()
        eight = pl.ds(p * 8, 8)
        density = dpart[eight, :]
        for j in range(15):
            density += dx[p, j]
        density = density * (1.0 / M)
        dens[eight, :] = density
        pot = vloc[eight, :] - (3.0 / jnp.pi) ** (1.0 / 3.0) * cbrt(density)
        turned = jnp.concatenate([pot, jnp.zeros((LINE - 8, LINE), jnp.float32)], axis=0).T
        for n in range(8):
            rows = pl.ds((p * 8 + n) * LINE, LINE)
            r = rotated[rows, :]
            h = hpsi[rows, :] + jnp.broadcast_to(turned[:, n:n + 1], (LINE, NORB)) * r
            hpsi[rows, :] = h
            acc += jnp.sum((r * h).reshape(LINE // 8, 8, NORB), axis=0)
    bpart[...] = acc
    for p in range(3):
        from_all(dx.at[p], d_send.at[p], d_recv.at[p], orb_peers).wait_send()
    to_all(bpart, bx, b_send.at[0], b_recv.at[0], dom_peers)
    shared = from_all(bx, b_send.at[0], b_recv.at[0], dom_peers)
    shared.wait_recv()
    total = acc
    for j in range(15):
        total += bx[j]
    band[...] = jnp.sum(total, axis=0, keepdims=True) * (1.0 / NPTS)
    shared.wait_send()

    for j in range(3):
        rot_1(j).wait_send()
        for n in range(2):
            rot_2(j, n).wait_send()
        remote(p2.at[0], p2.at[0], rs_send.at[j], rs_recv.at[0, 0], x_peers[j]).wait_send()
    for j in range(7):
        share_1(j).wait_send()
    share_2.wait_send()
    for side in range(2):
        remote(halo.at[0], halo.at[0], h_send.at[side], h_recv.at[0], at_next).wait_send()


def put_kernel(*refs):
    count = len(refs) // 2
    sem = refs[-1]
    copies = [pltpu.make_async_copy(refs[n], refs[count + n], sem.at[n]) for n in range(count)]
    for copy in copies:
        copy.start()
    for copy in copies:
        copy.wait()


def put(*arrays):
    hbm = pl.BlockSpec(memory_space=pl.ANY)
    return pl.pallas_call(
        put_kernel,
        out_shape=tuple(jax.ShapeDtypeStruct(a.shape, a.dtype) for a in arrays),
        in_specs=[hbm] * len(arrays),
        out_specs=(hbm,) * len(arrays),
        scratch_shapes=[pltpu.SemaphoreType.DMA((len(arrays),))],
        compiler_params=pltpu.CompilerParams(vmem_limit_bytes=16 * 1024 * 1024),
        name="put",
    )(*arrays)


def shards(psi, rot, occ, v_loc):
    f32 = jnp.float32
    vmem, hbm = pl.BlockSpec(memory_space=pltpu.VMEM), pl.BlockSpec(memory_space=pltpu.HBM)
    dma = pltpu.SemaphoreType.DMA
    rotated, density, hpsi, band = pl.pallas_call(
        kernel,
        out_shape=(
            jax.ShapeDtypeStruct((PTS, NORB), f32),
            jax.ShapeDtypeStruct((NLINE, LINE), f32),
            jax.ShapeDtypeStruct((PTS, NORB), f32),
            jax.ShapeDtypeStruct((1, NORB), f32),
        ),
        in_specs=[hbm] * 4,
        out_specs=(vmem, vmem, vmem, vmem),
        scratch_shapes=[
            pltpu.VMEM((1, NORB), f32),
            pltpu.VMEM((NLINE, LINE), f32),
            pltpu.VMEM((4, HALF, NORB), f32),
            pltpu.VMEM((4, HALF, NORB), f32),
            pltpu.VMEM((M, NORB), f32),
            pltpu.VMEM((8, 3, 64, NORB), f32),
            pltpu.VMEM((2, 3, 2, 128, NORB), f32),
            pltpu.VMEM((512, 512), jnp.bfloat16),
            pltpu.VMEM((512, 512), jnp.bfloat16),
            pltpu.VMEM((512, 512), jnp.bfloat16),
            pltpu.VMEM((512, 512), jnp.bfloat16),
            pltpu.VMEM((4, HALF, NORB), f32),
            pltpu.VMEM((4, HALF, NORB), f32),
            pltpu.VMEM((4, HALF, NORB), f32),
            pltpu.VMEM((4, HALF, NORB), f32),
            pltpu.VMEM((3, HALF, NORB), f32),
            pltpu.VMEM((2, 1024, NORB), f32),
            pltpu.VMEM((NLINE, LINE), f32),
            pltpu.VMEM((3, 15, 8, LINE), f32),
            pltpu.VMEM((8, NORB), f32),
            pltpu.VMEM((15, 8, NORB), f32),
            dma((6,)),
            dma((4, N)),
            dma((3,)),
            dma((4, N)),
            dma((2, 4)),
            dma((3,)),
            dma((3,)),
            dma((7,)),
            dma((8,)),
            dma((3, 2)),
            dma((3, 2)),
            dma((2,)),
            dma((4, N)),
            dma((4,)),
            dma((4, N)),
            dma((4,)),
            dma((3, N)),
            dma((3,)),
            dma((2,)),
            dma((2,)),
            dma((3,)),
            dma((3,)),
            dma((1,)),
            dma((1,)),
        ],
        compiler_params=pltpu.CompilerParams(
            collective_id=0, has_side_effects=True, vmem_limit_bytes=40 * 1024 * 1024),
        name="rotate",
    )(*[pltpu.with_memory_space_constraint(v, pltpu.HBM) for v in (
        psi, rot, occ.reshape(1, NORB), v_loc.reshape(NLINE, LINE))])
    return put(rotated, density.reshape(PTS), hpsi, band.reshape(NORB))


def solution(mesh):
    placed = (P("dom", "orb"), P(None, "orb"), P("orb"), P("dom"))
    return jax.shard_map(
        shards,
        mesh=mesh,
        in_specs=placed,
        out_specs=(P("dom", "orb"), P("dom"), P("dom", "orb"), P("orb")),
        check_vma=False,
    )
```

```python
import jax
import jax.numpy as jnp
from jax import lax
from jax.experimental import pallas as pl
from jax.experimental.pallas import tpu as pltpu
from jax.sharding import PartitionSpec as P

M = 2048
TINY = 1.1754944e-38
PTS = 3072
NORB = 128
NLINE = 24
LINE = 128
NPTS = 49152
N = 12
HALF = N * LINE
AHEAD1 = 3
AHEAD2 = 5
LAG_1 = 2
HOP = 1
DONE_1 = LAG_1 + 3 * HOP
LAG_2 = 3
DONE_2 = 4
LATE_1 = 4
LATE_2 = 5

MESH = pl.DeviceIdType.MESH
HIGHEST = lax.Precision.HIGHEST


def line_2(k):
    return k + 16 - 12 * (k // 8)


def split(v):
    hi = v.astype(jnp.bfloat16)
    return hi, (v - hi.astype(jnp.float32)).astype(jnp.bfloat16)


def cbrt(d):
    safe = jnp.maximum(d, TINY)
    y = jnp.exp(jnp.log(safe) * (1.0 / 3.0))
    y = y - (y - safe / (y * y)) * (1.0 / 3.0)
    return jnp.where(d < TINY, 0.0, y)


def kernel(psi, rot, occ_hbm, vloc_hbm, rotated, dens, hpsi, band,
           occ, vloc, a1, a2, rotv, rb1, rb2, b1hi, b1lo, b2hi, b2lo, q, into_r, into_l, p2, rs2, halo, dpart, dx, bpart, bx,
           in_sem, a1_recv, a1_send, a2_recv, a2_send, r1_send, r1_recv, s1_send, s1_recv, r2_send, r2_recv, s2_sem,
           r_recv, r_send, l_recv, l_send, rs_recv, rs_send, h_recv, h_send, d_send, d_recv, b_send, b_recv):
    dom = lax.axis_index("dom")
    orb = lax.axis_index("orb")
    y, zh, c = dom // 4, (dom // 2) % 2, dom % 2
    z, x = orb // 4, orb % 4
    at_right, at_left = (dom, ((z + 1) % 4) * 4 + x), (dom, ((z + 3) % 4) * 4 + x)
    at_prev, at_next = ((dom + 15) % 16, orb), ((dom + 1) % 16, orb)
    at_twin = (dom + 1 - 2 * c, orb)
    e = y * 2 + c

    def at_yc(f):
        return ((f // 2) * 4 + zh * 2 + f % 2, orb)

    x_peers = [(dom, z * 4 + (x + j) % 4) for j in (1, 2, 3)]
    z_peers = [(dom, ((z + j) % 4) * 4 + x) for j in (1, 2, 3)]
    orb_peers = [(dom, (orb + j) % 16) for j in range(1, 16)]
    dom_peers = [((dom + j) % 16, orb) for j in range(1, 16)]
    yc_peers = [at_yc((e + j) % 8) for j in range(1, 8)]

    loads = [pltpu.make_async_copy(src, dst, in_sem.at[n]) for n, (src, dst) in enumerate([
        (psi.at[pl.ds(0, HALF)], a1.at[x]),
        (psi.at[pl.ds(2048, 1024)], a2.at[z, pl.ds(0, 1024)]),
        (psi.at[pl.ds(HALF, 512)], a2.at[z, pl.ds(1024, 512)]),
        (rot, rotv), (occ_hbm, occ), (vloc_hbm, vloc)])]
    for load in loads:
        load.start()

    barrier = pltpu.get_barrier_semaphore()
    everyone = orb_peers + dom_peers
    for peer in everyone:
        pl.semaphore_signal(barrier, inc=1, device_id=peer, device_id_type=MESH)
    pl.semaphore_wait(barrier, len(everyone))
    for load in loads:
        load.wait()

    def remote(src, dst, send, recv, peer):
        return pltpu.make_async_remote_copy(
            src_ref=src, dst_ref=dst, send_sem=send, recv_sem=recv, device_id=peer, device_id_type=MESH)

    def at(n, size):
        return pl.ds(pl.multiple_of(n * size, size), size)

    def send_1(k):
        ref = a1.at[x, at(k, LINE)]
        for j in range(3):
            remote(ref, ref, a1_send.at[j], a1_recv.at[x, k], x_peers[j]).start()

    def block_2(b, k, way):
        ref = a2.at[b, at(k, LINE)]
        return remote(ref, ref, a2_send.at[way, b], a2_recv.at[b, k], at_left if way else at_right)

    def got_2(b, k):
        block_2(b, k, 0).wait_recv()

    def send_2(k):
        @pl.when(z < 3)
        def _():
            block_2(z, k, 0).start()

        @pl.when(z > 0)
        def _():
            block_2(z, k, 1).start()

    def rot_1(j):
        return remote(rotv.at[at(((z + j + 1) % 4) * 8 + e, 64)], rb1.at[e, 2 - j],
                      r1_send.at[j], r1_recv.at[2 - j], z_peers[j])

    def share_1(j):
        return remote(rb1.at[e], rb1.at[e], s1_send.at[j], s1_recv.at[e], yc_peers[j])

    def rot_2(j, n):
        return remote(rotv.at[at((2 * c + n) * 4 + (x + j + 1) % 4, 128)], rb2.at[c, 2 - j, n],
                      r2_send.at[j, n], r2_recv.at[2 - j, n], x_peers[j])

    share_2 = remote(rb2.at[c], rb2.at[c], s2_sem.at[0], s2_sem.at[1], at_twin)

    send_2(0)
    for j in range(3):
        rot_1(j).start()
    for j in range(3):
        for n in range(2):
            rot_2(j, n).start()
    for k in range(1, AHEAD2):
        send_2(k)
    for k in range(AHEAD1):
        send_1(k)

    def onward(t, k, way):
        rows = at(k, LINE)
        if way == 0:
            return remote(q.at[t, rows], into_r.at[t, rows], r_send.at[t], r_recv.at[t, k], at_right)
        return remote(q.at[t, rows], into_l.at[t, rows], l_send.at[t], l_recv.at[t, k], at_left)

    def rs_2(j, k):
        rows = at(k, LINE)
        return remote(p2.at[(x + j + 1) % 4, rows], rs2.at[2 - j, rows], rs_send.at[j], rs_recv.at[2 - j, k], x_peers[j])

    def to_all(src, dst, send, recv, peers):
        for j, peer in enumerate(peers):
            remote(src, dst.at[14 - j], send, recv, peer).start()

    def from_all(dst, send, recv, peers):
        return remote(dst, dst, send, recv, peers[0])

    def plane_sums(p):
        to_all(dpart.at[pl.ds(p * 8, 8)], dx.at[p], d_send.at[p], d_recv.at[p], orb_peers)

    def product(a, hi_ref, lo_ref):
        hi, lo = split(a)
        total = jnp.dot(hi, lo_ref[...], preferred_element_type=jnp.float32)
        total += jnp.dot(lo, hi_ref[...], preferred_element_type=jnp.float32)
        return total + jnp.dot(hi, hi_ref[...], preferred_element_type=jnp.float32)

    def finish(r, line):
        rotated[at(line, LINE), :] = r
        d = lax.dot_general(jnp.broadcast_to(occ[...], (8, NORB)), r * r, (((1,), (1,)), ((), ())),
                            precision=HIGHEST, preferred_element_type=jnp.float32)
        dpart[pl.ds(line, 1), :] = d[0:1]

    def valid(k):
        return (k >= 0) & (k < N)

    def step(i, _):
        for hop in (1, 2):
            k = i - hop + 1

            @pl.when(valid(k) & (z >= hop))
            def _(hop=hop, k=k):
                got_2(z - hop, k)

                @pl.when(z < 3)
                def _():
                    block_2(z - hop, k, 0).start()

            @pl.when(valid(k) & (z <= 3 - hop))
            def _(hop=hop, k=k):
                got_2(z + hop, k)

                @pl.when(z > 0)
                def _():
                    block_2(z + hop, k, 1).start()

        @pl.when(i == 0)
        def _():
            for j in range(3):
                rot_1(j).wait_recv()
            for j in range(7):
                share_1(j).start()

        @pl.when(i == 1)
        def _():
            for j in range(3):
                for n in range(2):
                    rot_2(j, n).wait_recv()
            share_2.start()

        @pl.when(i == LAG_2)
        def _():
            share_2.wait_recv()
            for n in range(4):
                hi, lo = split(rotv[at(n * 4 + x, 128), :])
                b2hi[pl.ds(n * 128, 128), at(x, 128)] = hi
                b2lo[pl.ds(n * 128, 128), at(x, 128)] = lo
            for j in range(3):
                hi, lo = split(rb2[:, j].reshape(512, NORB))
                b2hi[:, at((x + j + 1) % 4, 128)] = hi
                b2lo[:, at((x + j + 1) % 4, 128)] = lo

        @pl.when(i == LAG_1)
        def _():
            for j in range(1, 8):
                f = (e + j) % 8
                remote(rb1.at[f], rb1.at[f], s1_send.at[0], s1_recv.at[f], at_twin).wait_recv()
            hi, lo = split(rotv[at(z, 512), :])
            b1hi[:, at(z, 128)] = hi
            b1lo[:, at(z, 128)] = lo
            for j in range(3):
                hi, lo = split(rb1[:, j].reshape(512, NORB))
                b1hi[:, at((z + j + 1) % 4, 128)] = hi
                b1lo[:, at((z + j + 1) % 4, 128)] = lo

        k1 = i - LAG_1

        @pl.when(valid(k1))
        def _():
            for j in range(1, 4):
                b = (x + j) % 4
                ref = a1.at[b, at(k1, LINE)]
                remote(ref, ref, a1_send.at[0], a1_recv.at[b, k1], at_right).wait_recv()
            rows = at(k1, LINE)
            total = product(jnp.concatenate([a1[b, rows, :] for b in range(4)], axis=1), b1hi, b1lo)
            for t in range(4):
                q[t, rows, :] = total[:, t * 128:(t + 1) * 128]

        k_r, k_l = k1 - z * HOP, k1 - (3 - z) * HOP
        for t in range(4):
            for way, k, first, mine, into in ((0, k_r, z > 0, t > z, into_r), (1, k_l, z < 3, t < z, into_l)):
                @pl.when(valid(k) & first & mine)
                def _(t=t, way=way, k=k, into=into):
                    onward(t, k, way).wait_recv()
                    rows = at(k, LINE)
                    q[t, rows, :] = q[t, rows, :] + into[t, rows, :]

        k2 = i - LAG_2

        @pl.when(valid(k2))
        def _():
            @pl.when(z == 3)
            def _():
                got_2(0, k2)

            @pl.when(z == 0)
            def _():
                got_2(3, k2)

            rows = at(k2, LINE)
            total = product(jnp.concatenate([a2[b, rows, :] for b in range(4)], axis=1), b2hi, b2lo)
            for t in range(4):
                p2[t, rows, :] = total[:, t * 128:(t + 1) * 128]

        for t in range(4):
            for way, k, mine in ((0, k_r, (t > z) & (z < 3)), (1, k_l, (t < z) & (z > 0))):
                @pl.when(valid(k) & mine)
                def _(t=t, way=way, k=k):
                    onward(t, k, way).start()

        @pl.when(i + AHEAD2 < N)
        def _():
            send_2(i + AHEAD2)

        @pl.when(i + AHEAD1 < N)
        def _():
            send_1(i + AHEAD1)

        f1, f2 = i - DONE_1, i - DONE_2

        g1, g2 = f1 - LATE_1, f2 - LATE_2

        @pl.when((g1 >= 0) & (g1 < 8))
        def _():
            ref = at(g1, LINE)
            remote(rotated.at[ref], halo.at[1, ref], h_send.at[0], h_recv.at[1], at_prev).start()

        @pl.when((g2 >= 0) & (g2 < 8))
        def _():
            remote(rotated.at[at(g2 + 16, LINE)], halo.at[0, at(g2, LINE)],
                   h_send.at[1], h_recv.at[0], at_next).start()

        @pl.when(f1 == 8)
        def _():
            plane_sums(0)

        @pl.when(f2 == 8)
        def _():
            plane_sums(2)

        @pl.when(valid(f2))
        def _():
            rows = at(f2, LINE)
            for j in range(3):
                rs_2(j, f2).wait_recv()
            finish((p2[x, rows, :] + rs2[0, rows, :]) + (rs2[1, rows, :] + rs2[2, rows, :]), line_2(f2))

        @pl.when(valid(f1))
        def _():
            rows = at(f1, LINE)

            @pl.when(z > 0)
            def _():
                onward(z, f1, 0).wait_recv()
                q[z, rows, :] = q[z, rows, :] + into_r[z, rows, :]

            @pl.when(z < 3)
            def _():
                onward(z, f1, 1).wait_recv()
                q[z, rows, :] = q[z, rows, :] + into_l[z, rows, :]

            finish(q[z, rows, :], f1)

        @pl.when(valid(k2))
        def _():
            for j in range(3):
                rs_2(j, k2).start()

        return 0

    lax.fori_loop(0, max(N + DONE_1, 8 + DONE_1 + LATE_1, 8 + DONE_2 + LATE_2), step, 0)

    half = pl.ds(0, HALF)
    for j in range(3):
        remote(a1.at[x], a1.at[x], a1_send.at[j], a1_recv.at[0, 0], x_peers[j]).wait_send()
    for b in range(4):
        for way, out, on in ((0, (z < 3) & (b <= z), (z < 3) & (b > z)), (1, (z > 0) & (b >= z), (z > 0) & (b < z))):
            @pl.when(out)
            def _(b=b, way=way):
                remote(a2.at[b], a2.at[b], a2_send.at[way, b], a2_recv.at[0, 0], at_right).wait_send()

            @pl.when(on)
            def _(b=b, way=way):
                sem = l_send if way else r_send
                remote(q.at[b], q.at[b], sem.at[b], r_recv.at[0, 0], at_right).wait_send()

    plane_sums(1)

    remote(halo.at[0], halo.at[0], h_send.at[0], h_recv.at[0], at_next).wait_recv()
    remote(halo.at[1], halo.at[1], h_send.at[0], h_recv.at[1], at_next).wait_recv()

    for p in range(3):
        for line in range(8):
            rows = pl.ds(line * LINE, LINE)
            here = pl.ds((p * 8 + line) * LINE, LINE)
            r = rotated[here, :]
            total = rotated[pl.ds(((p - 1) * 8 + line) * LINE, LINE), :] if p > 0 else halo[0, rows, :]
            total += rotated[pl.ds(((p + 1) * 8 + line) * LINE, LINE), :] if p < 2 else halo[1, rows, :]
            total += rotated[pl.ds((p * 8 + (line + 1) % 8) * LINE, LINE), :]
            total += rotated[pl.ds((p * 8 + (line + 7) % 8) * LINE, LINE), :]
            total += pltpu.roll(r, 1, 0) + pltpu.roll(r, LINE - 1, 0)
            hpsi[here, :] = 3.0 * r - 0.5 * total

    acc = jnp.zeros((8, NORB), jnp.float32)
    for p in (0, 2, 1):
        from_all(dx.at[p], d_send.at[p], d_recv.at[p], orb_peers).wait_recv()
        eight = pl.ds(p * 8, 8)
        density = dpart[eight, :]
        for j in range(15):
            density += dx[p, j]
        density = density * (1.0 / M)
        dens[eight, :] = density
        pot = vloc[eight, :] - (3.0 / jnp.pi) ** (1.0 / 3.0) * cbrt(density)
        turned = jnp.concatenate([pot, jnp.zeros((LINE - 8, LINE), jnp.float32)], axis=0).T
        for n in range(8):
            rows = pl.ds((p * 8 + n) * LINE, LINE)
            r = rotated[rows, :]
            h = hpsi[rows, :] + jnp.broadcast_to(turned[:, n:n + 1], (LINE, NORB)) * r
            hpsi[rows, :] = h
            acc += jnp.sum((r * h).reshape(LINE // 8, 8, NORB), axis=0)
    bpart[...] = acc
    for p in range(3):
        from_all(dx.at[p], d_send.at[p], d_recv.at[p], orb_peers).wait_send()
    to_all(bpart, bx, b_send.at[0], b_recv.at[0], dom_peers)
    shared = from_all(bx, b_send.at[0], b_recv.at[0], dom_peers)
    shared.wait_recv()
    total = acc
    for j in range(15):
        total += bx[j]
    band[...] = jnp.sum(total, axis=0, keepdims=True) * (1.0 / NPTS)
    shared.wait_send()

    for j in range(3):
        rot_1(j).wait_send()
        for n in range(2):
            rot_2(j, n).wait_send()
        remote(p2.at[0], p2.at[0], rs_send.at[j], rs_recv.at[0, 0], x_peers[j]).wait_send()
    for j in range(7):
        share_1(j).wait_send()
    share_2.wait_send()
    for side in range(2):
        remote(halo.at[0], halo.at[0], h_send.at[side], h_recv.at[0], at_next).wait_send()


def put_kernel(*refs):
    count = len(refs) // 2
    sem = refs[-1]
    copies = [pltpu.make_async_copy(refs[n], refs[count + n], sem.at[n]) for n in range(count)]
    for copy in copies:
        copy.start()
    for copy in copies:
        copy.wait()


def put(*arrays):
    hbm = pl.BlockSpec(memory_space=pl.ANY)
    return pl.pallas_call(
        put_kernel,
        out_shape=tuple(jax.ShapeDtypeStruct(a.shape, a.dtype) for a in arrays),
        in_specs=[hbm] * len(arrays),
        out_specs=(hbm,) * len(arrays),
        scratch_shapes=[pltpu.SemaphoreType.DMA((len(arrays),))],
        compiler_params=pltpu.CompilerParams(vmem_limit_bytes=16 * 1024 * 1024),
        name="put",
    )(*arrays)


def shards(psi, rot, occ, v_loc):
    f32 = jnp.float32
    vmem, hbm = pl.BlockSpec(memory_space=pltpu.VMEM), pl.BlockSpec(memory_space=pltpu.HBM)
    dma = pltpu.SemaphoreType.DMA
    rotated, density, hpsi, band = pl.pallas_call(
        kernel,
        out_shape=(
            jax.ShapeDtypeStruct((PTS, NORB), f32),
            jax.ShapeDtypeStruct((NLINE, LINE), f32),
            jax.ShapeDtypeStruct((PTS, NORB), f32),
            jax.ShapeDtypeStruct((1, NORB), f32),
        ),
        in_specs=[hbm] * 4,
        out_specs=(vmem, vmem, vmem, vmem),
        scratch_shapes=[
            pltpu.VMEM((1, NORB), f32),
            pltpu.VMEM((NLINE, LINE), f32),
            pltpu.VMEM((4, HALF, NORB), f32),
            pltpu.VMEM((4, HALF, NORB), f32),
            pltpu.VMEM((M, NORB), f32),
            pltpu.VMEM((8, 3, 64, NORB), f32),
            pltpu.VMEM((2, 3, 2, 128, NORB), f32),
            pltpu.VMEM((512, 512), jnp.bfloat16),
            pltpu.VMEM((512, 512), jnp.bfloat16),
            pltpu.VMEM((512, 512), jnp.bfloat16),
            pltpu.VMEM((512, 512), jnp.bfloat16),
            pltpu.VMEM((4, HALF, NORB), f32),
            pltpu.VMEM((4, HALF, NORB), f32),
            pltpu.VMEM((4, HALF, NORB), f32),
            pltpu.VMEM((4, HALF, NORB), f32),
            pltpu.VMEM((3, HALF, NORB), f32),
            pltpu.VMEM((2, 1024, NORB), f32),
            pltpu.VMEM((NLINE, LINE), f32),
            pltpu.VMEM((3, 15, 8, LINE), f32),
            pltpu.VMEM((8, NORB), f32),
            pltpu.VMEM((15, 8, NORB), f32),
            dma((6,)),
            dma((4, N)),
            dma((3,)),
            dma((4, N)),
            dma((2, 4)),
            dma((3,)),
            dma((3,)),
            dma((7,)),
            dma((8,)),
            dma((3, 2)),
            dma((3, 2)),
            dma((2,)),
            dma((4, N)),
            dma((4,)),
            dma((4, N)),
            dma((4,)),
            dma((3, N)),
            dma((3,)),
            dma((2,)),
            dma((2,)),
            dma((3,)),
            dma((3,)),
            dma((1,)),
            dma((1,)),
        ],
        compiler_params=pltpu.CompilerParams(
            collective_id=0, has_side_effects=True, vmem_limit_bytes=40 * 1024 * 1024),
        name="rotate",
    )(*[pltpu.with_memory_space_constraint(v, pltpu.HBM) for v in (
        psi, rot, occ.reshape(1, NORB), v_loc.reshape(NLINE, LINE))])
    return put(rotated, density.reshape(PTS), hpsi, band.reshape(NORB))


def solution(mesh):
    placed = (P("dom", "orb"), P(None, "orb"), P("orb"), P("dom"))
    return jax.shard_map(
        shards,
        mesh=mesh,
        in_specs=placed,
        out_specs=(P("dom", "orb"), P("dom"), P("dom", "orb"), P("orb")),
        check_vma=False,
    )
```
